32 devices in a mesh: wide: 16 (over z, y, core), blk: 2 (over x).
Axes of the slice: x: 2, y: 2, z: 4, core: 2. Of those that a mesh axis runs over, the one named last changes fastest.
Arguments:
- position: float32 [3, 4096], P(None, ('wide', 'blk')), may hold values from -1 to 1, as said below
- order_field: float32 [12, 4096], P(None, ('wide', 'blk')), may hold values from -1.5 to 1.5
- cell_area: float32 [4096], P(('wide', 'blk')), may hold values from 0.5 to 2
- slot_vertex: int32 [16, 2, 16, 24], P('wide', 'blk'), may hold values from 0 to 127
- send_count: int32 [16, 2, 16], P('wide', 'blk'), may hold values from 0 to 24, as said below
- corner_slot: int32 [16, 2, 3, 256], P('wide', 'blk'), may hold values from 0 to 383, as said below
- edge_weight: float32 [16, 2, 3, 256], P('wide', 'blk'), may hold values from 0.2 to 2
Outputs:
- potential: float32 [12, 4096], P(None, ('wide', 'blk'))
The draws below stay inside these ranges and needn't reach their ends.
Inputs may be any that keep to these rules, and one draw needn't show every extreme that they name: `position`: each column is a unit vector. `slot_vertex`: slots of a block at or beyond the matching send_count are padding and hold arbitrary numbers. send_count[p, b, q] is how many leading slots of block [p, b, q] are live. It is nonzero exactly when (q - p) mod 16 is one of 0, 1, 2, 8, 15, 14, and then at least 12; every owner keeps all 24 slots live for one of the five requesters with (q - p) mod 16 among 0, 1, 2, 15, 14. `corner_slot`: A value c of requester (q, b) names slot c % 24 of owner (c // 24, b); it is always a live slot, and every live slot is named by some corner.
All inputs are finite; a program needn't handle non-finite values.
Results may differ from the reference program's by a relative error of at most 0.0003.
Values sent between devices are 32-bit elements; how exact they have to be, the bound alone decides.
A program may use at most 64 MiB of HBM per device.

```python
import functools
import math
import jax
import jax.numpy as jnp
from jax import lax

V_DEV = 128
SLOTS = 24
ELEM_DEV = 256
FIELDS = 12
VERTS = 4096
N_WIDE = 16
N_BLK = 2


def sphere_points(key):
    raw_normal = jax.random.normal(jax.random.fold_in(key, 101), (3, VERTS), jnp.float32)
    length = jnp.sqrt(jnp.sum(raw_normal * raw_normal, axis=0, keepdims=True) + 1e-12)
    return raw_normal / length


def pair_counts(key):
    lowest = max(1, SLOTS // 2)
    base_count = jax.random.randint(jax.random.fold_in(key, 303), (N_WIDE, N_BLK, N_WIDE), lowest, SLOTS + 1)
    owner_ids = jnp.arange(N_WIDE, dtype=jnp.int32)
    offset_map = (owner_ids[None, None, :] - owner_ids[:, None, None]) % N_WIDE
    nearby = (offset_map <= 2) | (offset_map >= N_WIDE - 2) | (offset_map == N_WIDE // 2)
    full_pick = jax.random.randint(jax.random.fold_in(key, 304), (N_WIDE, N_BLK), -2, 3)
    full_rank = (owner_ids[:, None] + full_pick) % N_WIDE
    forced = owner_ids[None, None, :] == full_rank[:, :, None]
    return jnp.where(forced, SLOTS, jnp.where(nearby, base_count, 0)).astype(jnp.int32)


def draw_position(key, part):
    return sphere_points(key)


def draw_order_field(key, part):
    ramp_line = 0.3 + 0.6 * jnp.arange(VERTS, dtype=jnp.float32) / VERTS
    noise_key = jax.random.fold_in(key, 202)
    rough = 0.4 * jax.random.normal(noise_key, (FIELDS, VERTS), jnp.float32)
    values = ramp_line[None, :] + rough
    return jnp.clip(values, -1.5, 1.5)


def draw_send_count(key, part):
    return pair_counts(key)


def draw_corner_slot(key, part):
    counts = pair_counts(key)
    needed = jnp.transpose(counts, (2, 1, 0))
    flat_slot = jnp.arange(N_WIDE * SLOTS, dtype=jnp.int32)
    live_int = ((flat_slot % SLOTS)[None, None, :] < jnp.repeat(needed, SLOTS, axis=2)).astype(jnp.int32)
    live_total = jnp.sum(live_int, axis=2)
    ordering = jnp.argsort(1 - live_int, axis=2, stable=True).astype(jnp.int32)
    key_list = jax.random.split(jax.random.fold_in(key, 405), N_WIDE * N_BLK)
    shuffles = jax.vmap(lambda one_key: jax.random.permutation(one_key, 3 * ELEM_DEV))(key_list)
    shuffles = shuffles.reshape(N_WIDE, N_BLK, 3 * ELEM_DEV).astype(jnp.int32)
    choose = shuffles % live_total[:, :, None]
    chosen = jnp.take_along_axis(ordering, choose, axis=2)
    return chosen.reshape(N_WIDE, N_BLK, 3, ELEM_DEV).astype(jnp.int32)


def touch_ends(entries, stream_key, smallest, top_value):
    longest = entries.shape.index(max(entries.shape))
    spots = []
    for shift in (0, 1):
        where = [jax.random.randint(jax.random.fold_in(stream_key, axis), (), 0, length) for axis, length in enumerate(entries.shape)]
        where[longest] = (where[longest] + shift) % entries.shape[longest]
        spots.append(tuple(where))
    return entries.at[spots[0]].set(smallest).at[spots[1]].set(top_value)


def block_scale(own_key, shape, cuts, least, top_value):
    def one(dim, blocks):
        heights = jax.random.uniform(jax.random.fold_in(jax.random.fold_in(own_key, 6), dim), (blocks,), jnp.float32, least / len(cuts), top_value / len(cuts))
        return jnp.repeat(jnp.exp(heights), shape[dim] // blocks).reshape((-1,) + (1,) * (len(shape) - dim - 1))

    factor_of = one(*cuts[0])
    for cut in cuts[1:]:
        factor_of = factor_of * one(*cut)
    return factor_of


def setup_inputs(seed: int = 0) -> dict:
    splits = jax.random.split(jax.random.key(seed), 8)
    return {
        "position": draw_position(jax.random.fold_in(splits[7], 71), 0),
        "order_field": draw_order_field(jax.random.fold_in(splits[7], 71), 0),
        "cell_area": jnp.clip(jnp.exp(math.log(2.0) - 1.3862944 * jax.random.uniform(splits[2], (VERTS,), jnp.float32) ** block_scale(splits[2], (VERTS,), ((0, 32),), -0.2, 0.2)), 0.5, 2.0),
        "slot_vertex": touch_ends(jax.random.randint(splits[3], (N_WIDE, N_BLK, N_WIDE, SLOTS), 0, V_DEV), jax.random.fold_in(splits[3], 1), 0, V_DEV - 1).astype(jnp.int32),
        "send_count": draw_send_count(jax.random.fold_in(splits[7], 71), 0),
        "corner_slot": draw_corner_slot(jax.random.fold_in(splits[7], 71), 0),
        "edge_weight": jnp.clip(jnp.exp(math.log(2.0) - 2.3025851 * jax.random.uniform(splits[6], (N_WIDE, N_BLK, 3, ELEM_DEV), jnp.float32) ** block_scale(splits[6], (N_WIDE, N_BLK, 3, ELEM_DEV), ((0, 16), (1, 2)), -0.2, 0.2)), 0.2, 2.0),
    }


stiff_coef = 0.1
source_block = 2048


def kernel_sum(targets, sources, weights, soften):
    number = sources.shape[1]
    block_len = math.gcd(number, source_block)

    def add_block(block_id, running):
        first_col = block_id * block_len
        source_pos = lax.dynamic_slice_in_dim(sources, first_col, block_len, 1)
        source_mass = lax.dynamic_slice_in_dim(weights, first_col, block_len, 1)
        distance = (targets[0][:, None] - source_pos[0][None, :]) ** 2
        distance = distance + (targets[1][:, None] - source_pos[1][None, :]) ** 2
        distance = distance + (targets[2][:, None] - source_pos[2][None, :]) ** 2
        kernel = jnp.log(distance + soften)
        return running + jnp.einsum("fs,ts->ft", source_mass, kernel, precision=lax.Precision.HIGHEST)

    start_sum = jnp.zeros((weights.shape[0], targets.shape[1]), jnp.float32)
    return lax.fori_loop(0, number // block_len, add_block, start_sum)


def corner_terms(values, weights):
    value_a, value_b, value_c = values[..., 0, :], values[..., 1, :], values[..., 2, :]
    weight_a, weight_b, weight_c = weights[..., 0, :], weights[..., 1, :], weights[..., 2, :]
    term_a = weight_c * (value_a - value_b) + weight_b * (value_a - value_c)
    term_b = weight_c * (value_b - value_a) + weight_a * (value_b - value_c)
    term_c = weight_b * (value_c - value_a) + weight_a * (value_c - value_b)
    return jnp.stack([term_a, term_b, term_c], axis=-2)


def reference(position, order_field, cell_area, slot_vertex, send_count, corner_slot, edge_weight):
    vertex_total = position.shape[1]
    fields = order_field.shape[0]
    average = jnp.sum(cell_area[None, :] * order_field, axis=1) / jnp.sum(cell_area)
    masses = cell_area[None, :] * (order_field - average[:, None])
    soften = 4.0 / vertex_total
    block_len = math.gcd(vertex_total, 128)
    tiles = position.reshape(3, vertex_total // block_len, block_len).transpose(1, 0, 2)
    runner = functools.partial(kernel_sum, sources=position, weights=masses, soften=soften)
    pieces = lax.map(runner, tiles)
    summed = pieces.transpose(1, 0, 2).reshape(fields, vertex_total)
    long_range = -(vertex_total ** -0.5) * summed

    wide_count = slot_vertex.shape[0]
    blk_count = slot_vertex.shape[1]
    slot_len = slot_vertex.shape[3]
    per_device = vertex_total // (wide_count * blk_count)
    owner_id = (corner_slot // slot_len).astype(jnp.int32)
    within = (corner_slot % slot_len).astype(jnp.int32)
    requester = jnp.arange(wide_count, dtype=jnp.int32)[:, None, None, None]
    column = jnp.arange(blk_count, dtype=jnp.int32)[None, :, None, None]
    local_id = slot_vertex[owner_id, column, requester, within]
    live_slot = within < send_count[owner_id, column, requester]
    global_id = ((owner_id * blk_count + column) * per_device + local_id).astype(jnp.int32)
    values = jnp.where(live_slot[None], order_field[:, global_id], 0.0)
    corner_sum = jnp.where(live_slot[None], corner_terms(values, edge_weight), 0.0)
    stiffness = jnp.zeros((fields, vertex_total), jnp.float32).at[:, global_id.reshape(-1)].add(
        corner_sum.reshape(fields, -1))
    return order_field ** 3 - order_field + stiff_coef * stiffness / cell_area[None, :] + long_range
```

```python
import functools

import jax
import jax.numpy as jnp
from jax import lax
from jax.experimental import pallas as pl
from jax.experimental.pallas import tpu as pltpu
from jax.sharding import PartitionSpec as P

stiff_coef = 0.1
LANES = 128
PAD = 32
GROUP = 4
FIRST = 2
MESH = pl.DeviceIdType.MESH
NT = (((1,), (1,)), ((), ()))
NN = (((1,), (0,)), ((), ()))


def halves(x):
    hi = x.astype(jnp.bfloat16)
    lo = (x - hi.astype(jnp.float32)).astype(jnp.bfloat16)
    return hi, lo


def stacked(x):
    return jnp.concatenate(halves(x), axis=0)


def mm(a, b, dims):
    return lax.dot_general(a, b, dims, preferred_element_type=jnp.float32)


def kernel(
    wide, blk, fields, slot_len,
    pos_hbm, order_hbm, area_hbm, slot_hbm, count_hbm, corner_hbm, weight_hbm,
    out_ref,
    pos_ref, order_ref, area_ref, slot_ref, count_ref, corner_ref, weight_ref,
    mine, blocks, vout, vbuf, rout, rbuf, targets,
    load_sem, own_sem, send_sem, block_sem, vsend, vrecv, rsend, rrecv, ready,
):
    n = wide * blk
    groups = n // GROUP
    my_w, my_b = lax.axis_index("wide"), lax.axis_index("blk")
    me = my_w * blk + my_b
    rows = fields + 4
    soften = 4.0 / (n * LANES)
    strength = float(n * LANES) ** (-0.5)
    offsets = (1, wide - 1, 2, wide - 2, wide // 2)
    total_slots = LANES + PAD

    def load(source, held, sem):
        return pltpu.make_async_copy(source, held, sem)

    own_loads = [
        load(source, held, own_sem.at[i])
        for i, (source, held) in enumerate((
            (order_hbm, order_ref), (pos_hbm, pos_ref), (area_hbm, area_ref),
        ))
    ]
    mesh_loads = [
        load(source, held, load_sem.at[i])
        for i, (source, held) in enumerate((
            (slot_hbm, slot_ref), (count_hbm, count_ref), (corner_hbm, corner_ref), (weight_hbm, weight_ref),
        ))
    ]
    for item in own_loads + mesh_loads:
        item.start()
    barrier = pltpu.get_barrier_semaphore()

    def greet_wide(step, carry):
        to = lax.rem(my_w + step, wide)
        pl.semaphore_signal(barrier, inc=1, device_id=(to, my_b), device_id_type=MESH)
        return carry

    def greet_blk(step, carry):
        to = lax.rem(my_b + step, blk)
        pl.semaphore_signal(barrier, inc=1, device_id=(my_w, to), device_id_type=MESH)
        return carry

    def tell_blk(step, carry):
        to = lax.rem(my_b + step, blk)
        pl.semaphore_signal(ready, inc=1, device_id=(my_w, to), device_id_type=MESH)
        return carry

    lax.fori_loop(1, blk, greet_blk, 0)
    lax.fori_loop(1, wide, greet_wide, 0)

    for item in own_loads:
        item.wait()
    own = jnp.concatenate([order_ref[...], pos_ref[...], area_ref[...]], axis=0)
    area = area_ref[...]
    mine[...] = own

    def block_copy(to_w, to_b):
        return pltpu.make_async_remote_copy(
            src_ref=mine, dst_ref=blocks.at[me], send_sem=send_sem,
            recv_sem=block_sem.at[me // GROUP], device_id=(to_w, to_b), device_id_type=MESH,
        )

    def send_range(first, last, to_b):
        def one(to_w, carry):
            @pl.when((to_w != my_w) | (to_b != my_b))
            def _():
                block_copy(to_w, to_b).start()
            return carry

        lax.fori_loop(first, last, one, 0)

    pl.semaphore_wait(barrier, wide + blk - 2)
    lax.fori_loop(1, blk, tell_blk, 0)

    @pl.when(my_b != 0)
    def _():
        pl.semaphore_wait(ready, blk - 1)

    send_range(0, FIRST, 0)
    pltpu.make_async_copy(mine, blocks.at[me], block_sem.at[me // GROUP]).start()

    for item in mesh_loads[:2]:
        item.wait()
    slot_row = lax.broadcasted_iota(jnp.int32, (slot_len, slot_len), 0)
    slot_lane = lax.broadcasted_iota(jnp.int32, (slot_len, slot_len), 1)
    slot_column = lax.broadcasted_iota(jnp.int32, (slot_len, 1), 0).astype(jnp.float32)
    count_lane = lax.broadcasted_iota(jnp.int32, (1, wide), 1)
    vertex_lane = lax.broadcasted_iota(jnp.int32, (slot_len, LANES), 1).astype(jnp.float32)
    count = count_ref[0].astype(jnp.float32)
    places = []
    for offset in offsets + (0,):
        to = lax.rem(my_w + offset, wide)
        row = slot_ref[0, 0, pl.ds(to, 1), :].astype(jnp.float32)
        vertex = jnp.sum(jnp.where(slot_row == slot_lane, row, 0.0), axis=1, keepdims=True)
        live = jnp.sum(jnp.where(count_lane == to, count, 0.0), axis=1, keepdims=True)
        vertex = jnp.where(slot_column < live, vertex, -1.0)
        places.append(jnp.where(vertex_lane == vertex, 1.0, 0.0))
    gap = [jnp.zeros((LANES - 5 * slot_len, LANES), jnp.float32)] if LANES > 5 * slot_len else []
    rest = [jnp.zeros((PAD - slot_len, LANES), jnp.float32)] if PAD > slot_len else []
    place = jnp.concatenate(places[:5] + gap + places[5:] + rest, axis=0).astype(jnp.bfloat16)
    outgoing = mm(stacked(own), place, NT)
    outgoing = outgoing[:rows] + outgoing[rows:]
    vout[...] = outgoing[:, :LANES]
    own_values = outgoing[:, LANES:]

    def value_copy(k):
        return pltpu.make_async_remote_copy(
            src_ref=vout, dst_ref=vbuf.at[k], send_sem=vsend, recv_sem=vrecv,
            device_id=(lax.rem(my_w + offsets[k], wide), my_b), device_id_type=MESH,
        )

    def term_copy(k):
        return pltpu.make_async_remote_copy(
            src_ref=rout, dst_ref=rbuf.at[k], send_sem=rsend, recv_sem=rrecv,
            device_id=(lax.rem(my_w + wide - offsets[k], wide), my_b), device_id_type=MESH,
        )

    for k in range(5):
        value_copy(k).start()

    send_range(jnp.where(my_b == 0, FIRST, 0), wide, my_b)

    for item in mesh_loads[2:]:
        item.wait()
    corner_rows = []
    for c in range(3):
        corner = corner_ref[c]
        column = jnp.full(corner.shape, -1, jnp.int32)
        for k, offset in enumerate(offsets + (0,)):
            low = lax.rem(my_w + wide - offset, wide) * slot_len
            first = k * slot_len if offset else LANES
            column = jnp.where((corner >= low) & (corner < low + slot_len), corner - low + first, column)
        corner_rows.append(column)
    column_id = lax.broadcasted_iota(jnp.int32, (total_slots, 1), 0)
    picks = [jnp.where(column_id == column, 1.0, 0.0) for column in corner_rows]
    signs, heavy, light = [], [], []
    for c in range(3):
        edge = picks[(c + 1) % 3] - picks[(c + 2) % 3]
        hi, lo = (half.astype(jnp.float32) for half in halves(weight_ref[c]))
        signs.append(edge.astype(jnp.bfloat16))
        heavy.append((edge * hi).astype(jnp.bfloat16))
        light.append((edge * lo).astype(jnp.bfloat16))
    signs = jnp.concatenate(signs, axis=1)
    matrix = mm(jnp.concatenate(heavy, axis=1), signs, NT)
    matrix = matrix + mm(jnp.concatenate(light, axis=1), signs, NT)
    matrix_high, matrix_low = halves(matrix)

    @pl.when(my_b == 0)
    def _():
        pl.semaphore_wait(ready, blk - 1)

    def send_part(step, carry):
        to_b = lax.rem(my_b + step, blk)
        send_range(jnp.where(to_b == 0, FIRST, 0), wide, to_b)
        return carry

    lax.fori_loop(1, blk, send_part, 0)

    columns = own.T
    for k in range(3):
        targets[k] = jnp.broadcast_to(columns[:, fields + k:fields + k + 1], (LANES, LANES))
    row_id = lax.broadcasted_iota(jnp.int32, (rows, 1), 0)
    center = jnp.sum(own * area, axis=1, keepdims=True) / jnp.sum(area)
    center = jnp.where(row_id < fields, center, 0.0)
    factor_row = row_id < fields

    def add_group(group, carry):
        acc, sums = carry
        first = group * GROUP
        held = blocks.at[pl.ds(first, GROUP)]
        pltpu.make_async_copy(held, held, block_sem.at[group]).wait()
        his, los, weights = [], [], []
        for u in range(GROUP):
            block = blocks[first + u]
            distance = (targets[0] - block[fields:fields + 1]) ** 2
            distance = distance + (targets[1] - block[fields + 1:fields + 2]) ** 2
            distance = distance + (targets[2] - block[fields + 2:fields + 3]) ** 2
            hi, lo = halves(jnp.log(distance + soften))
            mass = (block - center) * jnp.where(factor_row, block[fields + 3:], 1.0)
            sums = sums + mass
            his.append(hi)
            los.append(lo)
            weights.append(stacked(mass))
        weight = jnp.concatenate(weights, axis=1)
        acc = acc + mm(jnp.concatenate(his, axis=1), weight, NT)
        acc = acc + mm(jnp.concatenate(los, axis=1), weight, NT)
        return acc, sums

    part_lane = lax.broadcasted_iota(jnp.int32, (1, LANES), 1)

    def merged(buffer):
        total = jnp.zeros((rows, LANES), jnp.float32)
        for k in range(5):
            inside = (part_lane >= k * slot_len) & (part_lane < (k + 1) * slot_len)
            total = jnp.where(inside, buffer[k], total)
        return total

    early = jnp.where(my_w < FIRST, groups - 2, 0)
    carry = (jnp.zeros((LANES, 2 * rows), jnp.float32), jnp.zeros((rows, LANES), jnp.float32))
    carry = lax.fori_loop(0, early, add_group, carry)

    pltpu.make_async_copy(vbuf, vbuf, vrecv).wait()
    values = jnp.concatenate([merged(vbuf), own_values], axis=1)
    high, low = halves(values)
    returned = mm(jnp.concatenate([high, low], axis=0), matrix_high, NN)
    returned = returned[:rows] + returned[rows:] + mm(high, matrix_low, NN)
    rout[...] = returned[:, :LANES]
    own_terms = returned[:, LANES:]
    for k in range(5):
        term_copy(k).start()

    acc, sums = lax.fori_loop(early, groups, add_group, carry)

    pltpu.make_async_copy(rbuf, rbuf, rrecv).wait()
    back = jnp.concatenate([merged(rbuf), own_terms], axis=1)
    stiffness = mm(stacked(back), place, NN)
    stiffness = stiffness[:rows] + stiffness[rows:]
    total = acc.T
    total = total[:rows] + total[rows:]
    sums = jnp.sum(sums, axis=1, keepdims=True)
    shift = sums / sums[fields + 3:]
    long_range = -strength * (total - shift * total[fields + 3:])
    result = stiff_coef * stiffness / area + long_range
    out_ref[...] = result[:fields]

    sent = blocks.at[pl.ds(0, n - 1)]
    pltpu.make_async_copy(sent, sent, send_sem).wait()
    pltpu.make_async_copy(vbuf, vbuf, vsend).wait()
    pltpu.make_async_copy(rbuf, rbuf, rsend).wait()


def per_device(position, order_field, cell_area, slot_vertex, send_count, corner_slot, edge_weight):
    fields, local_count = order_field.shape
    wide, blk = lax.axis_size("wide"), lax.axis_size("blk")
    n = wide * blk
    rows = fields + 4
    slot_len = slot_vertex.shape[3]
    args = (
        position, order_field, cell_area.reshape(1, local_count), slot_vertex, send_count,
        corner_slot.reshape(3, 1, -1), edge_weight.reshape(3, 1, -1),
    )
    vmem = pl.BlockSpec(memory_space=pltpu.VMEM)
    dma = pltpu.SemaphoreType.DMA
    one = pltpu.SemaphoreType.DMA(())
    extra = pl.pallas_call(
        functools.partial(kernel, wide, blk, fields, slot_len),
        out_shape=pltpu.VMEM((fields, local_count), jnp.float32),
        in_specs=[pl.BlockSpec(memory_space=pl.ANY)] * 7,
        out_specs=vmem,
        scratch_shapes=[
            *(pltpu.VMEM(x.shape, x.dtype) for x in args),
            pltpu.VMEM((rows, LANES), jnp.float32),
            pltpu.VMEM((n, rows, LANES), jnp.float32),
            pltpu.VMEM((rows, LANES), jnp.float32),
            pltpu.VMEM((5, rows, LANES), jnp.float32),
            pltpu.VMEM((rows, LANES), jnp.float32),
            pltpu.VMEM((5, rows, LANES), jnp.float32),
            pltpu.VMEM((3, LANES, LANES), jnp.float32),
            dma((4,)), dma((3,)), one, dma((n // GROUP,)), one, one, one, one,
            pltpu.SemaphoreType.REGULAR,
        ],
        compiler_params=pltpu.CompilerParams(collective_id=0, has_side_effects=True),
    )(*args)
    return order_field**3 - order_field + extra


def solution(mesh):
    placed = (
        P(None, ("wide", "blk")),
        P(None, ("wide", "blk")),
        P(("wide", "blk")),
        P("wide", "blk", None, None),
        P("wide", "blk", None),
        P("wide", "blk", None, None),
        P("wide", "blk", None, None),
    )
    return jax.shard_map(
        per_device, mesh=mesh, in_specs=placed, out_specs=P(None, ("wide", "blk")), check_vma=False
    )
```

```python
import functools

import jax
import jax.numpy as jnp
from jax import lax
from jax.experimental import pallas as pl
from jax.experimental.pallas import tpu as pltpu
from jax.sharding import PartitionSpec as P

stiff_coef = 0.1
LANES = 128
PAD = 32
PLANES = 4
ID_ROWS = 2
ROWS = 176
MESH = pl.DeviceIdType.MESH
NT = (((1,), (1,)), ((), ()))
NN = (((1,), (0,)), ((), ()))


def halves(x):
    hi = x.astype(jnp.bfloat16)
    lo = (x - hi.astype(jnp.float32)).astype(jnp.bfloat16)
    return hi, lo


def stacked(x):
    return jnp.concatenate(halves(x), axis=0)


def mm(a, b, dims):
    return lax.dot_general(a, b, dims, preferred_element_type=jnp.float32)


def kernel(
    wide, blk, fields, slot_len,
    pos_hbm, order_hbm, area_hbm, slot_hbm, count_hbm, corner_hbm, weight_hbm,
    out_ref,
    pos_ref, order_ref, area_ref, slot_ref, count_ref, corner_ref, weight_ref,
    mine, mine_near, near, far, matrix_ref, matrices, values, targets, acc_ref, sums_ref, swap, swapped,
    load_sem, near_sem, far_sem, matrix_sem, sent_sem, swap_sem, ready,
):
    chips = wide // 2
    across = chips // 2
    per_plane = chips // PLANES
    total = chips * blk
    my_w, my_b = lax.axis_index("wide"), lax.axis_index("blk")
    core, chip = lax.rem(my_w, 2), my_w // 2
    sibling = my_w + 1 - 2 * core
    plane = chip // per_plane
    place_in_order = chip * blk + my_b
    rows = fields + 4
    soften = 4.0 / (wide * blk * LANES)
    strength = float(wide * blk * LANES) ** (-0.5)
    offsets = (1, wide - 1, 2, wide - 2, wide // 2)
    firsts = (LANES, LANES + slot_len, 0, slot_len, 2 * slot_len, 3 * slot_len)
    steps = (chips - 1, 1, across)

    loads = [
        pltpu.make_async_copy(source, held, load_sem.at[i])
        for i, (source, held) in enumerate((
            (order_hbm, order_ref), (pos_hbm, pos_ref), (area_hbm, area_ref), (slot_hbm, slot_ref),
            (count_hbm, count_ref), (corner_hbm, corner_ref), (weight_hbm, weight_ref),
        ))
    ]
    for load in loads:
        load.start()
    barrier = pltpu.get_barrier_semaphore()

    def device(index):
        return (2 * (index // blk) + core, lax.rem(index, blk))

    def loop(first, last, body):
        def step(i, carry):
            body(i)
            return carry

        lax.fori_loop(first, last, step, 0)

    def signal(semaphore, to):
        pl.semaphore_signal(semaphore, inc=1, device_id=to, device_id_type=MESH)

    other_chips = [lax.rem(chip + step, chips) for step in steps]

    loop(0, total - 1 - place_in_order, lambda i: signal(barrier, device(total - 1 - i)))
    signal(barrier, (sibling, my_b))
    for other in other_chips:
        @pl.when(other > chip)
        def _():
            signal(barrier, (2 * other + 1 - core, my_b))

    for load in loads[:3]:
        load.wait()
    own = jnp.concatenate([order_ref[...], pos_ref[...], area_ref[...]], axis=0)
    area = area_ref[...]
    mine[...] = own
    mine_near[:rows] = own

    def far_copy(to_chip, to_b):
        part = lax.rem(my_b - to_b + blk, blk) - 1
        slot = (plane * (blk - 1) + part) * per_plane + chip - plane * per_plane
        return pltpu.make_async_remote_copy(
            src_ref=mine, dst_ref=far.at[slot], send_sem=sent_sem.at[0], recv_sem=far_sem.at[plane],
            device_id=(2 * to_chip + core, to_b), device_id_type=MESH,
        )

    def near_copy(to_chip):
        return pltpu.make_async_remote_copy(
            src_ref=mine_near, dst_ref=near.at[chip], send_sem=sent_sem.at[1], recv_sem=near_sem.at[plane],
            device_id=(2 * to_chip + core, my_b), device_id_type=MESH,
        )

    earlier = place_in_order + 1
    for other in other_chips:
        earlier = earlier + jnp.where(other < chip, 1, 0)
    pl.semaphore_wait(barrier, earlier)

    def far_earlier(to_chip):
        def one(step):
            to_b = lax.rem(my_b + step, blk)
            signal(ready.at[plane], (2 * to_chip + core, to_b))
            far_copy(to_chip, to_b).start()

        loop(1, blk, one)
        signal(ready.at[plane], (2 * to_chip + core, my_b))

    def far_here(to_b):
        signal(ready.at[plane], (my_w, to_b))
        far_copy(chip, to_b).start()

    loop(0, chip, far_earlier)
    loop(0, my_b, far_here)
    for other in other_chips:
        @pl.when(other < chip)
        def _():
            signal(ready.at[plane], (2 * other + 1 - core, my_b))

    for load in loads[3:5]:
        load.wait()
    lane = lax.broadcasted_iota(jnp.int32, (1, 2 * LANES), 1)
    base = jnp.full((1, 2 * LANES), -1, jnp.int32)
    towards = jnp.full((1, 2 * LANES), -1, jnp.int32)
    for first, offset in zip(firsts, offsets + (0,)):
        inside = (lane >= first) & (lane < first + slot_len)
        base = jnp.where(inside, lane - first, base)
        towards = jnp.where(inside, lax.rem(my_w + offset, wide), towards)
    count_lane = lax.broadcasted_iota(jnp.int32, (wide, wide), 1)
    count_row = lax.broadcasted_iota(jnp.int32, (wide, wide), 0)
    counts = count_ref[0].astype(jnp.float32)
    counts = jnp.sum(jnp.where(count_lane == count_row, counts, 0.0), axis=1, keepdims=True)
    slot_id = lax.broadcasted_iota(jnp.int32, (wide, slot_len), 1).astype(jnp.float32)
    table = jnp.where(slot_id < counts, slot_ref[0, 0].astype(jnp.float32) + 1.0, 0.0)
    spread_row = lax.broadcasted_iota(jnp.int32, (slot_len, 2 * LANES), 0)
    spread = jnp.where(spread_row == base, 1.0, 0.0).astype(jnp.bfloat16)
    spread_table = mm(table.astype(jnp.bfloat16), spread, NN)
    wide_row = lax.broadcasted_iota(jnp.int32, (wide, 2 * LANES), 0)
    vertex_of = jnp.sum(jnp.where(wide_row == towards, spread_table, 0.0), axis=0, keepdims=True)
    mine_near[rows:rows + 1] = vertex_of[:, :LANES]
    mine_near[rows + 1:] = vertex_of[:, LANES:]
    loop(0, chip, lambda to_chip: near_copy(to_chip).start())
    sibling_copy = pltpu.make_async_remote_copy(
        src_ref=mine_near, dst_ref=near.at[chips], send_sem=sent_sem.at[1], recv_sem=near_sem.at[PLANES],
        device_id=(sibling, my_b), device_id_type=MESH,
    )
    sibling_copy.start()
    pltpu.make_async_copy(mine_near, near.at[chip], near_sem.at[plane]).start()

    for load in loads[5:]:
        load.wait()
    column_id = lax.broadcasted_iota(jnp.int32, (ROWS, 1), 0)
    picks = []
    for c in range(3):
        corner = corner_ref[c]
        column = jnp.full(corner.shape, -1, jnp.int32)
        for first, offset in zip(firsts, offsets + (0,)):
            low = lax.rem(my_w + wide - offset, wide) * slot_len
            column = jnp.where((corner >= low) & (corner < low + slot_len), corner - low + first, column)
        picks.append(jnp.where(column_id == column, 1.0, 0.0))
    signs, heavy, light = [], [], []
    for c in range(3):
        edge = picks[(c + 1) % 3] - picks[(c + 2) % 3]
        hi, lo = (half.astype(jnp.float32) for half in halves(weight_ref[c]))
        signs.append(edge.astype(jnp.bfloat16))
        heavy.append((edge * hi).astype(jnp.bfloat16))
        light.append((edge * lo).astype(jnp.bfloat16))
    signs = jnp.concatenate(signs, axis=1)
    matrix = mm(jnp.concatenate(heavy, axis=1), signs, NT)
    matrix = matrix + mm(jnp.concatenate(light, axis=1), signs, NT)
    matrix_ref[:, LANES:] = jnp.zeros_like(matrix_ref[:, LANES:])
    matrix_ref[:, :LANES] = matrix[:, :LANES]
    matrix_ref[:, LANES:ROWS] = matrix[:, LANES:]

    def matrix_rows(k, tile):
        return matrix_ref.at[pl.ds(firsts[k], slot_len), pl.ds(tile * LANES, LANES)]

    def matrix_copy(k, tile, to_chip):
        to_core = core if tile == 0 else 1 - core
        owner_core = core if k >= 2 else 1 - core
        return pltpu.make_async_remote_copy(
            src_ref=matrix_rows(k, tile), dst_ref=matrices.at[owner_core, k], send_sem=sent_sem.at[2],
            recv_sem=matrix_sem, device_id=(2 * to_chip + to_core, my_b), device_id_type=MESH,
        )

    owner_chips = [lax.rem(my_w + wide - offset, wide) // 2 for offset in offsets]
    for k in (0, 1, 5):
        @pl.when((k == 5) | (core == 1 - k))
        def _():
            owner_core = core if k >= 2 else 1 - core
            pltpu.make_async_copy(matrix_rows(k, 0), matrices.at[owner_core, k], matrix_sem).start()
            matrix_copy(k, 1, chip).start()

    def send_matrix(wanted):
        for k in range(5):
            @pl.when(wanted(owner_chips[k]))
            def _():
                for tile in range(2):
                    matrix_copy(k, tile, owner_chips[k]).start()

    send_matrix(lambda owner: owner < chip)

    def send_later(which):
        first = which * per_plane
        low = jnp.maximum(first, chip + 1)
        high = first + per_plane
        here = jnp.where(plane == which, blk - 1 - my_b, 0)
        later = jnp.maximum(high - low, 0) * blk + here
        for other in other_chips:
            later = later + jnp.where((other > chip) & (other // per_plane == which), 1, 0)

        @pl.when(later > 0)
        def _():
            pl.semaphore_wait(ready.at[which], later)
            loop(my_b + 1, my_b + 1 + here, lambda to_b: far_copy(chip, to_b).start())

            def one(i):
                to_chip = low + high - 1 - i
                near_copy(to_chip).start()
                loop(1, blk, lambda step: far_copy(to_chip, lax.rem(my_b + step, blk)).start())

            loop(low, high, one)
            send_matrix(lambda owner: (owner > chip) & (owner // per_plane == which))

    ascending = plane < PLANES // 2

    def plane_at(step):
        return jnp.where(ascending, step, PLANES - 1 - step)

    for step in range(PLANES):
        send_later(plane_at(step))

    def set_targets(which, held):
        columns = held.T
        for k in range(3):
            targets[which, k] = jnp.broadcast_to(columns[:, fields + k:fields + k + 1], (LANES, LANES))

    set_targets(0, own)
    row_id = lax.broadcasted_iota(jnp.int32, (rows, 1), 0)
    factor_row = row_id < fields
    center = jnp.sum(own * area, axis=1, keepdims=True) / jnp.sum(area)
    center = jnp.where(factor_row, center, 0.0)
    vertex_row = lax.broadcasted_iota(jnp.int32, (LANES, LANES), 0).astype(jnp.float32) + 1.0

    def placed(held):
        halves_of = [jnp.where(vertex_row == held[rows + i:rows + i + 1], 1.0, 0.0) for i in range(2)]
        return jnp.concatenate(halves_of, axis=1).astype(jnp.bfloat16)

    acc_ref[...] = jnp.zeros_like(acc_ref)
    sums_ref[...] = jnp.zeros_like(sums_ref)
    pltpu.make_async_copy(near.at[chips], near.at[chips], near_sem.at[PLANES]).wait()
    set_targets(1, near[chips, :rows])

    def add_pair(source, first):
        his, los, weights = [], [], []
        sums = sums_ref[...]
        for u in range(2):
            block = source[first + u, :rows]
            both = []
            for which in range(2):
                distance = (targets[which, 0] - block[fields:fields + 1]) ** 2
                distance = distance + (targets[which, 1] - block[fields + 1:fields + 2]) ** 2
                distance = distance + (targets[which, 2] - block[fields + 2:fields + 3]) ** 2
                both.append(halves(jnp.log(distance + soften)))
            mass = (block - center) * jnp.where(factor_row, block[fields + 3:], 1.0)
            sums = sums + mass
            his.append(jnp.concatenate([both[0][0], both[1][0]], axis=0))
            los.append(jnp.concatenate([both[0][1], both[1][1]], axis=0))
            weights.append(stacked(mass))
        sums_ref[...] = sums
        weight = jnp.concatenate(weights, axis=1)
        added = mm(jnp.concatenate(his, axis=1), weight, NT)
        acc_ref[...] += added + mm(jnp.concatenate(los, axis=1), weight, NT)

    def near_pair(pair):
        first = 2 * pair
        add_pair(near, first)
        for u in range(2):
            block = near[first + u]
            values[first + u] = mm(stacked(block[:rows]), placed(block), NN)

    def far_plane(which):
        number = (blk - 1) * per_plane
        held = far.at[pl.ds(which * number, number)]
        pltpu.make_async_copy(held, held, far_sem.at[which]).wait()
        loop(which * number // 2, (which + 1) * number // 2, lambda pair: add_pair(far, 2 * pair))

    def one_plane(step):
        which = plane_at(step)
        held = near.at[pl.ds(which * per_plane, per_plane)]
        pltpu.make_async_copy(held, held, near_sem.at[which]).wait()
        loop(which * per_plane // 2, (which + 1) * per_plane // 2, near_pair)

        @pl.when(step + 1 < PLANES)
        def _():
            far_plane(which)

    loop(0, PLANES, one_plane)

    part_lane = lax.broadcasted_iota(jnp.int32, (1, LANES), 1)
    group = [part_lane // slot_len == k for k in range(4)]
    same = [jnp.full((1, LANES), core, jnp.int32) == place for place in range(2)]

    def held_values(owner, tile):
        return values[lax.rem(owner + chips, chips), :, tile * LANES:(tile + 1) * LANES]

    used = {}
    for step, moved in enumerate((0, 1, chips - 1, across)):
        user = chip + moved
        even = jnp.where(group[0], held_values(user - 1, 0), jnp.where(group[1], held_values(user + 1, 0), 0.0))
        even = jnp.where(group[2], held_values(user + across, 0), jnp.where(group[3], held_values(user, 0), even))
        odd = jnp.where(group[0], held_values(user - core, 1), jnp.where(group[1], held_values(user + 1 - core, 1), 0.0))
        for place in range(2):
            used[step, place] = jnp.where(same[place], even, odd).astype(jnp.bfloat16)
    pairs = {
        (0, 0): ((0, 5), (1, 1)), (0, 1): ((0, 0), (1, 5)), (1, 0): ((0, 2), (1, 0)), (1, 1): ((1, 2),),
        (2, 0): ((0, 3),), (2, 1): ((0, 1), (1, 3)), (3, 0): ((0, 4),), (3, 1): ((1, 4),),
    }
    pltpu.make_async_copy(matrices, matrices, matrix_sem).wait()
    returned = {}
    for key, members in pairs.items():
        held = jnp.concatenate([matrices[owner, k] for owner, k in members], axis=0)
        count = held.shape[0]
        hi = held.astype(jnp.bfloat16).astype(jnp.float32)
        both = jnp.concatenate([hi, held - hi], axis=0).astype(jnp.bfloat16)
        result = mm(both, used[key][:rows], NT)
        result = result[:count] + result[count:] + mm(hi.astype(jnp.bfloat16), used[key][rows:], NT)
        for i, member in enumerate(members):
            returned[member] = result[i * slot_len:(i + 1) * slot_len]
    gap = jnp.zeros((LANES - 4 * slot_len, rows), jnp.float32)
    rest = jnp.zeros((LANES - 2 * slot_len, rows), jnp.float32)
    sides = [
        jnp.concatenate(
            [returned[to, k] for k in (2, 3, 4, 5)] + [gap] + [returned[to, k] for k in (0, 1)] + [rest], axis=0
        )
        for to in range(2)
    ]
    first_core = same[0][:, :rows]
    mine_terms = jnp.where(first_core, sides[0], sides[1])
    other_terms = jnp.where(first_core, sides[1], sides[0])

    def assembled(held, terms):
        place = placed(held)
        hi, lo = halves(terms)
        return (mm(place, hi, NN) + mm(place, lo, NN)).T

    stiffness = assembled(mine_near[...], mine_terms)
    other_stiffness = assembled(near[chips], other_terms)

    far_plane(plane_at(PLANES - 1))

    sums = jnp.sum(sums_ref[...], axis=1, keepdims=True)
    sums = sums + center * sums[fields + 3:]

    def summed(which):
        part = acc_ref[which * LANES:(which + 1) * LANES].T
        part = part[:rows] + part[rows:]
        return part + center * part[fields + 3:]

    swap[:rows] = summed(1)
    swap[rows:2 * rows] = jnp.broadcast_to(sums, (rows, LANES))
    swap[2 * rows:] = other_stiffness
    swap_copy = pltpu.make_async_remote_copy(
        src_ref=swap, dst_ref=swapped, send_sem=sent_sem.at[3], recv_sem=swap_sem,
        device_id=(sibling, my_b), device_id_type=MESH,
    )
    swap_copy.start()
    own_sum = summed(0)
    sent_far = far.at[pl.ds(0, chips * (blk - 1))]
    pltpu.make_async_copy(sent_far, sent_far, sent_sem.at[0]).wait()
    sent_near = near.at[pl.ds(0, chips)]
    pltpu.make_async_copy(sent_near, sent_near, sent_sem.at[1]).wait()
    for k in range(5):
        pltpu.make_async_copy(matrices.at[:, k], matrices.at[:, k], sent_sem.at[2]).wait()
    swap_copy.wait_recv()
    all_sum = own_sum + swapped[:rows]
    sums = sums + swapped[rows:2 * rows]
    stiffness = stiffness + swapped[2 * rows:]
    shift = sums / sums[fields + 3:]
    long_range = -strength * (all_sum - shift * all_sum[fields + 3:])
    result = stiff_coef * stiffness / area + long_range
    out_ref[...] = result[:fields]
    swap_copy.wait_send()


def per_device(position, order_field, cell_area, slot_vertex, send_count, corner_slot, edge_weight):
    fields, local_count = order_field.shape
    wide, blk = lax.axis_size("wide"), lax.axis_size("blk")
    rows = fields + 4
    chips = wide // 2
    slot_len = slot_vertex.shape[3]
    args = (
        position, order_field, cell_area.reshape(1, local_count), slot_vertex, send_count,
        corner_slot.reshape(3, 1, -1), edge_weight.reshape(3, 1, -1),
    )
    dma = pltpu.SemaphoreType.DMA
    extra = pl.pallas_call(
        functools.partial(kernel, wide, blk, fields, slot_len),
        out_shape=pltpu.VMEM((fields, local_count), jnp.float32),
        in_specs=[pl.BlockSpec(memory_space=pl.ANY)] * 7,
        out_specs=pl.BlockSpec(memory_space=pltpu.VMEM),
        scratch_shapes=[
            *(pltpu.VMEM(x.shape, x.dtype) for x in args),
            pltpu.VMEM((rows, LANES), jnp.float32),
            pltpu.VMEM((rows + ID_ROWS, LANES), jnp.float32),
            pltpu.VMEM((chips + 1, rows + ID_ROWS, LANES), jnp.float32),
            pltpu.VMEM((chips * (blk - 1), rows, LANES), jnp.float32),
            pltpu.VMEM((ROWS, 2 * LANES), jnp.float32),
            pltpu.VMEM((2, 6, slot_len, LANES), jnp.float32),
            pltpu.VMEM((chips, 2 * rows, 2 * LANES), jnp.float32),
            pltpu.VMEM((2, 3, LANES, LANES), jnp.float32),
            pltpu.VMEM((2 * LANES, 2 * rows), jnp.float32),
            pltpu.VMEM((rows, LANES), jnp.float32),
            pltpu.VMEM((3 * rows, LANES), jnp.float32),
            pltpu.VMEM((3 * rows, LANES), jnp.float32),
            dma((7,)), dma((PLANES + 1,)), dma((PLANES,)), dma(()), dma((4,)), dma(()),
            pltpu.SemaphoreType.REGULAR((PLANES,)),
        ],
        compiler_params=pltpu.CompilerParams(collective_id=0, has_side_effects=True),
    )(*args)
    return order_field**3 - order_field + extra


def solution(mesh):
    placed = (
        P(None, ("wide", "blk")),
        P(None, ("wide", "blk")),
        P(("wide", "blk")),
        P("wide", "blk", None, None),
        P("wide", "blk", None),
        P("wide", "blk", None, None),
        P("wide", "blk", None, None),
    )
    return jax.shard_map(
        per_device, mesh=mesh, in_specs=placed, out_specs=P(None, ("wide", "blk")), check_vma=False
    )
```

```python
import functools

import jax
import jax.numpy as jnp
from jax import lax
from jax.experimental import pallas as pl
from jax.experimental.pallas import tpu as pltpu
from jax.sharding import PartitionSpec as P

stiff_coef = 0.1
LANES = 128
PAD = 32
PLANES = 4
FIRST = 1
ID_ROWS = 2
ROWS = 176
MESH = pl.DeviceIdType.MESH
NT = (((1,), (1,)), ((), ()))
NN = (((1,), (0,)), ((), ()))


def halves(x):
    hi = x.astype(jnp.bfloat16)
    lo = (x - hi.astype(jnp.float32)).astype(jnp.bfloat16)
    return hi, lo


def stacked(x):
    return jnp.concatenate(halves(x), axis=0)


def mm(a, b, dims):
    return lax.dot_general(a, b, dims, preferred_element_type=jnp.float32)


def kernel(
    wide, blk, fields, slot_len,
    pos_hbm, order_hbm, area_hbm, slot_hbm, count_hbm, corner_hbm, weight_hbm,
    out_ref,
    pos_ref, order_ref, area_ref, slot_ref, count_ref, corner_ref, weight_ref,
    mine, mine_near, near, far, matrix_ref, matrices, values, targets, acc_ref, sums_ref, swap, swapped,
    load_sem, near_sem, far_sem, matrix_sem, sent_sem, swap_sem, ready,
):
    chips = wide // 2
    across = chips // 2
    per_plane = chips // PLANES
    total = chips * blk
    my_w, my_b = lax.axis_index("wide"), lax.axis_index("blk")
    core, chip = lax.rem(my_w, 2), my_w // 2
    sibling = my_w + 1 - 2 * core
    plane = chip // per_plane
    place_in_order = chip * blk + my_b
    rows = fields + 4
    soften = 4.0 / (wide * blk * LANES)
    strength = float(wide * blk * LANES) ** (-0.5)
    offsets = (1, wide - 1, 2, wide - 2, wide // 2)
    firsts = (LANES, LANES + slot_len, 0, slot_len, 2 * slot_len, 3 * slot_len)
    steps = (chips - 1, 1, across)

    loads = [
        pltpu.make_async_copy(source, held, load_sem.at[i])
        for i, (source, held) in enumerate((
            (order_hbm, order_ref), (pos_hbm, pos_ref), (area_hbm, area_ref), (slot_hbm, slot_ref),
            (count_hbm, count_ref), (corner_hbm, corner_ref), (weight_hbm, weight_ref),
        ))
    ]
    for load in loads:
        load.start()
    barrier = pltpu.get_barrier_semaphore()

    def device(index):
        return (2 * (index // blk) + core, lax.rem(index, blk))

    def loop(first, last, body):
        def step(i, carry):
            body(i)
            return carry

        lax.fori_loop(first, last, step, 0)

    def signal(semaphore, to):
        pl.semaphore_signal(semaphore, inc=1, device_id=to, device_id_type=MESH)

    other_chips = [lax.rem(chip + step, chips) for step in steps]

    loop(0, total - 1 - place_in_order, lambda i: signal(barrier, device(total - 1 - i)))
    signal(barrier, (sibling, my_b))
    for other in other_chips:
        @pl.when(other > chip)
        def _():
            signal(barrier, (2 * other + 1 - core, my_b))

    earlier = place_in_order + 1
    for other in other_chips:
        earlier = earlier + jnp.where(other < chip, 1, 0)
    pl.semaphore_wait(barrier, earlier)

    loop(0, place_in_order, lambda i: signal(ready.at[plane], device(i)))
    for other in other_chips:
        @pl.when(other < chip)
        def _():
            signal(ready.at[plane], (2 * other + 1 - core, my_b))

    for load in loads[:3]:
        load.wait()
    own = jnp.concatenate([order_ref[...], pos_ref[...], area_ref[...]], axis=0)
    area = area_ref[...]
    mine[...] = own
    mine_near[:rows] = own

    def far_copy(to_chip, to_b):
        part = lax.rem(my_b - to_b + blk, blk) - 1
        slot = (plane * (blk - 1) + part) * per_plane + chip - plane * per_plane
        return pltpu.make_async_remote_copy(
            src_ref=mine, dst_ref=far.at[slot], send_sem=sent_sem.at[0], recv_sem=far_sem.at[plane],
            device_id=(2 * to_chip + core, to_b), device_id_type=MESH,
        )

    def near_copy(to_chip):
        return pltpu.make_async_remote_copy(
            src_ref=mine_near, dst_ref=near.at[chip], send_sem=sent_sem.at[1], recv_sem=near_sem.at[plane],
            device_id=(2 * to_chip + core, my_b), device_id_type=MESH,
        )

    def far_earlier(to_chip):
        def one(step):
            to_b = lax.rem(my_b + step, blk)
            far_copy(to_chip, to_b).start()

        loop(1, blk, one)

    def far_here(to_b):
        far_copy(chip, to_b).start()

    loop(0, jnp.minimum(chip, FIRST), far_earlier)
    for load in loads[3:5]:
        load.wait()
    lane = lax.broadcasted_iota(jnp.int32, (1, 2 * LANES), 1)
    base = jnp.full((1, 2 * LANES), -1, jnp.int32)
    towards = jnp.full((1, 2 * LANES), -1, jnp.int32)
    for first, offset in zip(firsts, offsets + (0,)):
        inside = (lane >= first) & (lane < first + slot_len)
        base = jnp.where(inside, lane - first, base)
        towards = jnp.where(inside, lax.rem(my_w + offset, wide), towards)
    count_lane = lax.broadcasted_iota(jnp.int32, (wide, wide), 1)
    count_row = lax.broadcasted_iota(jnp.int32, (wide, wide), 0)
    counts = count_ref[0].astype(jnp.float32)
    counts = jnp.sum(jnp.where(count_lane == count_row, counts, 0.0), axis=1, keepdims=True)
    slot_id = lax.broadcasted_iota(jnp.int32, (wide, slot_len), 1).astype(jnp.float32)
    table = jnp.where(slot_id < counts, slot_ref[0, 0].astype(jnp.float32) + 1.0, 0.0)
    spread_row = lax.broadcasted_iota(jnp.int32, (slot_len, 2 * LANES), 0)
    spread = jnp.where(spread_row == base, 1.0, 0.0).astype(jnp.bfloat16)
    spread_table = mm(table.astype(jnp.bfloat16), spread, NN)
    wide_row = lax.broadcasted_iota(jnp.int32, (wide, 2 * LANES), 0)
    vertex_of = jnp.sum(jnp.where(wide_row == towards, spread_table, 0.0), axis=0, keepdims=True)
    mine_near[rows:rows + 1] = vertex_of[:, :LANES]
    mine_near[rows + 1:] = vertex_of[:, LANES:]
    loop(0, jnp.minimum(chip, FIRST), lambda to_chip: near_copy(to_chip).start())
    sibling_copy = pltpu.make_async_remote_copy(
        src_ref=mine_near, dst_ref=near.at[chips], send_sem=sent_sem.at[1], recv_sem=near_sem.at[PLANES],
        device_id=(sibling, my_b), device_id_type=MESH,
    )
    sibling_copy.start()
    pltpu.make_async_copy(mine_near, near.at[chip], near_sem.at[plane]).start()

    for load in loads[5:]:
        load.wait()
    column_id = lax.broadcasted_iota(jnp.int32, (ROWS, 1), 0)
    picks = []
    for c in range(3):
        corner = corner_ref[c]
        column = jnp.full(corner.shape, -1, jnp.int32)
        for first, offset in zip(firsts, offsets + (0,)):
            low = lax.rem(my_w + wide - offset, wide) * slot_len
            column = jnp.where((corner >= low) & (corner < low + slot_len), corner - low + first, column)
        picks.append(jnp.where(column_id == column, 1.0, 0.0))
    signs, heavy, light = [], [], []
    for c in range(3):
        edge = picks[(c + 1) % 3] - picks[(c + 2) % 3]
        hi, lo = (half.astype(jnp.float32) for half in halves(weight_ref[c]))
        signs.append(edge.astype(jnp.bfloat16))
        heavy.append((edge * hi).astype(jnp.bfloat16))
        light.append((edge * lo).astype(jnp.bfloat16))
    signs = jnp.concatenate(signs, axis=1)
    matrix = mm(jnp.concatenate(heavy, axis=1), signs, NT)
    matrix = matrix + mm(jnp.concatenate(light, axis=1), signs, NT)
    matrix_ref[:, LANES:] = jnp.zeros_like(matrix_ref[:, LANES:])
    matrix_ref[:, :LANES] = matrix[:, :LANES]
    matrix_ref[:, LANES:ROWS] = matrix[:, LANES:]

    def matrix_rows(k, tile):
        return matrix_ref.at[pl.ds(firsts[k], slot_len), pl.ds(tile * LANES, LANES)]

    def matrix_copy(k, tile, to_chip):
        to_core = core if tile == 0 else 1 - core
        owner_core = core if k >= 2 else 1 - core
        return pltpu.make_async_remote_copy(
            src_ref=matrix_rows(k, tile), dst_ref=matrices.at[owner_core, k], send_sem=sent_sem.at[2],
            recv_sem=matrix_sem, device_id=(2 * to_chip + to_core, my_b), device_id_type=MESH,
        )

    owner_chips = [lax.rem(my_w + wide - offset, wide) // 2 for offset in offsets]
    for k in (0, 1, 5):
        @pl.when((k == 5) | (core == 1 - k))
        def _():
            owner_core = core if k >= 2 else 1 - core
            pltpu.make_async_copy(matrix_rows(k, 0), matrices.at[owner_core, k], matrix_sem).start()
            matrix_copy(k, 1, chip).start()

    def send_matrix(wanted):
        for k in range(5):
            @pl.when(wanted(owner_chips[k]))
            def _():
                for tile in range(2):
                    matrix_copy(k, tile, owner_chips[k]).start()

    send_matrix(lambda owner: (owner < chip) & (owner < FIRST))

    def send_both(to_chip):
        far_earlier(to_chip)
        near_copy(to_chip).start()

    loop(FIRST, chip, send_both)
    loop(0, my_b, far_here)
    send_matrix(lambda owner: (owner < chip) & (owner >= FIRST))

    def send_later(which):
        first = which * per_plane
        low = jnp.maximum(first, chip + 1)
        high = first + per_plane
        here = jnp.where(plane == which, blk - 1 - my_b, 0)
        later = jnp.maximum(high - low, 0) * blk + here
        for other in other_chips:
            later = later + jnp.where((other > chip) & (other // per_plane == which), 1, 0)

        @pl.when(later > 0)
        def _():
            pl.semaphore_wait(ready.at[which], later)
            loop(my_b + 1, my_b + 1 + here, lambda to_b: far_copy(chip, to_b).start())

            def one(i):
                to_chip = i
                near_copy(to_chip).start()
                loop(1, blk, lambda step: far_copy(to_chip, lax.rem(my_b + step, blk)).start())

            loop(low, high, one)
            send_matrix(lambda owner: (owner > chip) & (owner // per_plane == which))

    ascending = plane < PLANES // 2

    def plane_at(step):
        return jnp.where(ascending, step, jnp.where(step < 2, PLANES - 1 - step, step - 2))


    def set_targets(which, held):
        columns = held.T
        for k in range(3):
            targets[which, k] = jnp.broadcast_to(columns[:, fields + k:fields + k + 1], (LANES, LANES))

    set_targets(0, own)
    row_id = lax.broadcasted_iota(jnp.int32, (rows, 1), 0)
    factor_row = row_id < fields
    center = jnp.sum(own * area, axis=1, keepdims=True) / jnp.sum(area)
    center = jnp.where(factor_row, center, 0.0)
    vertex_row = lax.broadcasted_iota(jnp.int32, (LANES, LANES), 0).astype(jnp.float32) + 1.0

    def placed(held):
        halves_of = [jnp.where(vertex_row == held[rows + i:rows + i + 1], 1.0, 0.0) for i in range(2)]
        return jnp.concatenate(halves_of, axis=1).astype(jnp.bfloat16)

    acc_ref[...] = jnp.zeros_like(acc_ref)
    sums_ref[...] = jnp.zeros_like(sums_ref)
    pltpu.make_async_copy(near.at[chips], near.at[chips], near_sem.at[PLANES]).wait()
    set_targets(1, near[chips, :rows])
    for step in range(PLANES):
        send_later(plane_at(step))

    def add_pair(source, first):
        his, los, weights = [], [], []
        sums = sums_ref[...]
        for u in range(2):
            block = source[first + u, :rows]
            both = []
            for which in range(2):
                distance = (targets[which, 0] - block[fields:fields + 1]) ** 2
                distance = distance + (targets[which, 1] - block[fields + 1:fields + 2]) ** 2
                distance = distance + (targets[which, 2] - block[fields + 2:fields + 3]) ** 2
                both.append(halves(jnp.log(distance + soften)))
            mass = (block - center) * jnp.where(factor_row, block[fields + 3:], 1.0)
            sums = sums + mass
            his.append(jnp.concatenate([both[0][0], both[1][0]], axis=0))
            los.append(jnp.concatenate([both[0][1], both[1][1]], axis=0))
            weights.append(stacked(mass))
        sums_ref[...] = sums
        weight = jnp.concatenate(weights, axis=1)
        added = mm(jnp.concatenate(his, axis=1), weight, NT)
        acc_ref[...] += added + mm(jnp.concatenate(los, axis=1), weight, NT)

    def near_pair(pair):
        first = 2 * pair
        add_pair(near, first)
        for u in range(2):
            block = near[first + u]
            values[first + u] = mm(stacked(block[:rows]), placed(block), NN)

    def far_plane(which):
        number = (blk - 1) * per_plane
        held = far.at[pl.ds(which * number, number)]
        pltpu.make_async_copy(held, held, far_sem.at[which]).wait()
        loop(which * number // 2, (which + 1) * number // 2, lambda pair: add_pair(far, 2 * pair))

    def one_plane(step):
        which = plane_at(step)
        held = near.at[pl.ds(which * per_plane, per_plane)]
        pltpu.make_async_copy(held, held, near_sem.at[which]).wait()
        loop(which * per_plane // 2, (which + 1) * per_plane // 2, near_pair)

        @pl.when(step + 1 < PLANES)
        def _():
            far_plane(which)

    loop(0, PLANES, one_plane)

    part_lane = lax.broadcasted_iota(jnp.int32, (1, LANES), 1)
    group = [part_lane // slot_len == k for k in range(4)]
    same = [jnp.full((1, LANES), core, jnp.int32) == place for place in range(2)]

    def held_values(owner, tile):
        return values[lax.rem(owner + chips, chips), :, tile * LANES:(tile + 1) * LANES]

    used = {}
    for step, moved in enumerate((0, 1, chips - 1, across)):
        user = chip + moved
        even = jnp.where(group[0], held_values(user - 1, 0), jnp.where(group[1], held_values(user + 1, 0), 0.0))
        even = jnp.where(group[2], held_values(user + across, 0), jnp.where(group[3], held_values(user, 0), even))
        odd = jnp.where(group[0], held_values(user - core, 1), jnp.where(group[1], held_values(user + 1 - core, 1), 0.0))
        for place in range(2):
            used[step, place] = jnp.where(same[place], even, odd).astype(jnp.bfloat16)
    pairs = {
        (0, 0): ((0, 5), (1, 1)), (0, 1): ((0, 0), (1, 5)), (1, 0): ((0, 2), (1, 0)), (1, 1): ((1, 2),),
        (2, 0): ((0, 3),), (2, 1): ((0, 1), (1, 3)), (3, 0): ((0, 4),), (3, 1): ((1, 4),),
    }
    pltpu.make_async_copy(matrices, matrices, matrix_sem).wait()
    returned = {}
    for key, members in pairs.items():
        held = jnp.concatenate([matrices[owner, k] for owner, k in members], axis=0)
        count = held.shape[0]
        hi = held.astype(jnp.bfloat16).astype(jnp.float32)
        both = jnp.concatenate([hi, held - hi], axis=0).astype(jnp.bfloat16)
        result = mm(both, used[key][:rows], NT)
        result = result[:count] + result[count:] + mm(hi.astype(jnp.bfloat16), used[key][rows:], NT)
        for i, member in enumerate(members):
            returned[member] = result[i * slot_len:(i + 1) * slot_len]
    gap = jnp.zeros((LANES - 4 * slot_len, rows), jnp.float32)
    rest = jnp.zeros((LANES - 2 * slot_len, rows), jnp.float32)
    sides = [
        jnp.concatenate(
            [returned[to, k] for k in (2, 3, 4, 5)] + [gap] + [returned[to, k] for k in (0, 1)] + [rest], axis=0
        )
        for to in range(2)
    ]
    first_core = same[0][:, :rows]
    mine_terms = jnp.where(first_core, sides[0], sides[1])
    other_terms = jnp.where(first_core, sides[1], sides[0])

    def assembled(held, terms):
        place = placed(held)
        hi, lo = halves(terms)
        return (mm(place, hi, NN) + mm(place, lo, NN)).T

    stiffness = assembled(mine_near[...], mine_terms)
    other_stiffness = assembled(near[chips], other_terms)

    far_plane(plane_at(PLANES - 1))

    sums = jnp.sum(sums_ref[...], axis=1, keepdims=True)
    sums = sums + center * sums[fields + 3:]

    def summed(which):
        part = acc_ref[which * LANES:(which + 1) * LANES].T
        part = part[:rows] + part[rows:]
        return part + center * part[fields + 3:]

    swap[:rows] = summed(1)
    swap[rows:2 * rows] = jnp.broadcast_to(sums, (rows, LANES))
    swap[2 * rows:] = other_stiffness
    swap_copy = pltpu.make_async_remote_copy(
        src_ref=swap, dst_ref=swapped, send_sem=sent_sem.at[3], recv_sem=swap_sem,
        device_id=(sibling, my_b), device_id_type=MESH,
    )
    swap_copy.start()
    own_sum = summed(0)
    sent_far = far.at[pl.ds(0, chips * (blk - 1))]
    pltpu.make_async_copy(sent_far, sent_far, sent_sem.at[0]).wait()
    sent_near = near.at[pl.ds(0, chips)]
    pltpu.make_async_copy(sent_near, sent_near, sent_sem.at[1]).wait()
    for k in range(5):
        pltpu.make_async_copy(matrices.at[:, k], matrices.at[:, k], sent_sem.at[2]).wait()
    swap_copy.wait_recv()
    all_sum = own_sum + swapped[:rows]
    sums = sums + swapped[rows:2 * rows]
    stiffness = stiffness + swapped[2 * rows:]
    shift = sums / sums[fields + 3:]
    long_range = -strength * (all_sum - shift * all_sum[fields + 3:])
    result = stiff_coef * stiffness / area + long_range
    out_ref[...] = result[:fields]
    swap_copy.wait_send()


def per_device(position, order_field, cell_area, slot_vertex, send_count, corner_slot, edge_weight):
    fields, local_count = order_field.shape
    wide, blk = lax.axis_size("wide"), lax.axis_size("blk")
    rows = fields + 4
    chips = wide // 2
    slot_len = slot_vertex.shape[3]
    args = (
        position, order_field, cell_area.reshape(1, local_count), slot_vertex, send_count,
        corner_slot.reshape(3, 1, -1), edge_weight.reshape(3, 1, -1),
    )
    dma = pltpu.SemaphoreType.DMA
    extra = pl.pallas_call(
        functools.partial(kernel, wide, blk, fields, slot_len),
        out_shape=pltpu.VMEM((fields, local_count), jnp.float32),
        in_specs=[pl.BlockSpec(memory_space=pl.ANY)] * 7,
        out_specs=pl.BlockSpec(memory_space=pltpu.VMEM),
        scratch_shapes=[
            *(pltpu.VMEM(x.shape, x.dtype) for x in args),
            pltpu.VMEM((rows, LANES), jnp.float32),
            pltpu.VMEM((rows + ID_ROWS, LANES), jnp.float32),
            pltpu.VMEM((chips + 1, rows + ID_ROWS, LANES), jnp.float32),
            pltpu.VMEM((chips * (blk - 1), rows, LANES), jnp.float32),
            pltpu.VMEM((ROWS, 2 * LANES), jnp.float32),
            pltpu.VMEM((2, 6, slot_len, LANES), jnp.float32),
            pltpu.VMEM((chips, 2 * rows, 2 * LANES), jnp.float32),
            pltpu.VMEM((2, 3, LANES, LANES), jnp.float32),
            pltpu.VMEM((2 * LANES, 2 * rows), jnp.float32),
            pltpu.VMEM((rows, LANES), jnp.float32),
            pltpu.VMEM((3 * rows, LANES), jnp.float32),
            pltpu.VMEM((3 * rows, LANES), jnp.float32),
            dma((7,)), dma((PLANES + 1,)), dma((PLANES,)), dma(()), dma((4,)), dma(()),
            pltpu.SemaphoreType.REGULAR((PLANES,)),
        ],
        compiler_params=pltpu.CompilerParams(collective_id=0, has_side_effects=True),
    )(*args)
    return order_field**3 - order_field + extra


def solution(mesh):
    placed = (
        P(None, ("wide", "blk")),
        P(None, ("wide", "blk")),
        P(("wide", "blk")),
        P("wide", "blk", None, None),
        P("wide", "blk", None),
        P("wide", "blk", None, None),
        P("wide", "blk", None, None),
    )
    return jax.shard_map(
        per_device, mesh=mesh, in_specs=placed, out_specs=P(None, ("wide", "blk")), check_vma=False
    )
```

```python
import functools

import jax
import jax.numpy as jnp
from jax import lax
from jax.experimental import pallas as pl
from jax.experimental.pallas import tpu as pltpu
from jax.sharding import PartitionSpec as P

stiff_coef = 0.1
LANES = 128
PAD = 32
PLANES = 4
FIRST = 1
ID_ROWS = 2
ROWS = 176
MESH = pl.DeviceIdType.MESH
NT = (((1,), (1,)), ((), ()))
NN = (((1,), (0,)), ((), ()))


def halves(x):
    hi = x.astype(jnp.bfloat16)
    lo = (x - hi.astype(jnp.float32)).astype(jnp.bfloat16)
    return hi, lo


def stacked(x):
    return jnp.concatenate(halves(x), axis=0)


def mm(a, b, dims):
    return lax.dot_general(a, b, dims, preferred_element_type=jnp.float32)


def kernel(
    wide, blk, fields, slot_len,
    pos_hbm, order_hbm, area_hbm, slot_hbm, count_hbm, corner_hbm, weight_hbm,
    out_ref,
    pos_ref, order_ref, area_ref, slot_ref, count_ref, corner_ref, weight_ref,
    mine, mine_near, near, far, matrix_ref, matrices, values, targets, acc_ref, sums_ref, swap, swapped,
    load_sem, near_sem, far_sem, matrix_sem, sent_sem, swap_sem, ready,
):
    chips = wide // 2
    across = chips // 2
    per_plane = chips // PLANES
    total = chips * blk
    my_w, my_b = lax.axis_index("wide"), lax.axis_index("blk")
    core, chip = lax.rem(my_w, 2), my_w // 2
    side = 1 - core
    sibling = 2 * chip + side
    plane = chip // per_plane
    place_in_order = chip * blk + my_b
    rows = fields + 4
    soften = 4.0 / (wide * blk * LANES)
    strength = float(wide * blk * LANES) ** (-0.5)
    offsets = (1, wide - 1, 2, wide - 2, wide // 2)
    firsts = (LANES, LANES + slot_len, 0, slot_len, 2 * slot_len, 3 * slot_len)
    steps = (chips - 1, 1, across)

    loads = [
        pltpu.make_async_copy(source, held, load_sem.at[i])
        for i, (source, held) in enumerate((
            (order_hbm, order_ref), (pos_hbm, pos_ref), (area_hbm, area_ref), (slot_hbm, slot_ref),
            (count_hbm, count_ref), (corner_hbm, corner_ref), (weight_hbm, weight_ref),
        ))
    ]
    for load in loads:
        load.start()
    barrier = pltpu.get_barrier_semaphore()

    def device(index):
        return (2 * (index // blk) + side, lax.rem(index, blk))

    def loop(first, last, body):
        def step(i, carry):
            body(i)
            return carry

        lax.fori_loop(first, last, step, 0)

    def signal(semaphore, to):
        pl.semaphore_signal(semaphore, inc=1, device_id=to, device_id_type=MESH)

    other_chips = [lax.rem(chip + step, chips) for step in steps]

    loop(0, total - 1 - place_in_order, lambda i: signal(barrier, device(total - 1 - i)))
    signal(barrier, (sibling, my_b))
    for other in other_chips:
        @pl.when(other > chip)
        def _():
            signal(barrier, (2 * other + core, my_b))

    earlier = place_in_order + 1
    for other in other_chips:
        earlier = earlier + jnp.where(other < chip, 1, 0)
    pl.semaphore_wait(barrier, earlier)

    loop(0, place_in_order, lambda i: signal(ready.at[plane], device(i)))
    for other in other_chips:
        @pl.when(other < chip)
        def _():
            signal(ready.at[plane], (2 * other + core, my_b))

    for load in loads[:3]:
        load.wait()
    own = jnp.concatenate([order_ref[...], pos_ref[...], area_ref[...]], axis=0)
    area = area_ref[...]
    mine[...] = own
    mine_near[:rows] = own

    def far_copy(to_chip, to_b):
        part = lax.rem(my_b - to_b + blk, blk) - 1
        slot = (plane * (blk - 1) + part) * per_plane + chip - plane * per_plane
        return pltpu.make_async_remote_copy(
            src_ref=mine, dst_ref=far.at[slot], send_sem=sent_sem.at[0], recv_sem=far_sem.at[plane],
            device_id=(2 * to_chip + side, to_b), device_id_type=MESH,
        )

    def near_copy(to_chip):
        return pltpu.make_async_remote_copy(
            src_ref=mine_near, dst_ref=near.at[chip], send_sem=sent_sem.at[1], recv_sem=near_sem.at[plane],
            device_id=(2 * to_chip + side, my_b), device_id_type=MESH,
        )

    def far_earlier(to_chip):
        def one(step):
            to_b = lax.rem(my_b + step, blk)
            far_copy(to_chip, to_b).start()

        loop(1, blk, one)

    def far_here(to_b):
        far_copy(chip, to_b).start()

    loop(0, jnp.minimum(chip, FIRST), far_earlier)
    for load in loads[3:5]:
        load.wait()
    lane = lax.broadcasted_iota(jnp.int32, (1, 2 * LANES), 1)
    base = jnp.full((1, 2 * LANES), -1, jnp.int32)
    towards = jnp.full((1, 2 * LANES), -1, jnp.int32)
    for first, offset in zip(firsts, offsets + (0,)):
        inside = (lane >= first) & (lane < first + slot_len)
        base = jnp.where(inside, lane - first, base)
        towards = jnp.where(inside, lax.rem(my_w + offset, wide), towards)
    count_lane = lax.broadcasted_iota(jnp.int32, (wide, wide), 1)
    count_row = lax.broadcasted_iota(jnp.int32, (wide, wide), 0)
    counts = count_ref[0].astype(jnp.float32)
    counts = jnp.sum(jnp.where(count_lane == count_row, counts, 0.0), axis=1, keepdims=True)
    slot_id = lax.broadcasted_iota(jnp.int32, (wide, slot_len), 1).astype(jnp.float32)
    table = jnp.where(slot_id < counts, slot_ref[0, 0].astype(jnp.float32) + 1.0, 0.0)
    spread_row = lax.broadcasted_iota(jnp.int32, (slot_len, 2 * LANES), 0)
    spread = jnp.where(spread_row == base, 1.0, 0.0).astype(jnp.bfloat16)
    spread_table = mm(table.astype(jnp.bfloat16), spread, NN)
    wide_row = lax.broadcasted_iota(jnp.int32, (wide, 2 * LANES), 0)
    vertex_of = jnp.sum(jnp.where(wide_row == towards, spread_table, 0.0), axis=0, keepdims=True)
    mine_near[rows:rows + 1] = vertex_of[:, :LANES]
    mine_near[rows + 1:] = vertex_of[:, LANES:]
    loop(0, jnp.minimum(chip, FIRST), lambda to_chip: near_copy(to_chip).start())
    sibling_copy = pltpu.make_async_remote_copy(
        src_ref=mine_near, dst_ref=near.at[chips], send_sem=sent_sem.at[1], recv_sem=near_sem.at[PLANES],
        device_id=(sibling, my_b), device_id_type=MESH,
    )
    sibling_copy.start()
    near_copy(chip).start()

    for load in loads[5:]:
        load.wait()
    column_id = lax.broadcasted_iota(jnp.int32, (ROWS, 1), 0)
    picks = []
    for c in range(3):
        corner = corner_ref[c]
        column = jnp.full(corner.shape, -1, jnp.int32)
        for first, offset in zip(firsts, offsets + (0,)):
            low = lax.rem(my_w + wide - offset, wide) * slot_len
            column = jnp.where((corner >= low) & (corner < low + slot_len), corner - low + first, column)
        picks.append(jnp.where(column_id == column, 1.0, 0.0))
    signs, heavy, light = [], [], []
    for c in range(3):
        edge = picks[(c + 1) % 3] - picks[(c + 2) % 3]
        hi, lo = (half.astype(jnp.float32) for half in halves(weight_ref[c]))
        signs.append(edge.astype(jnp.bfloat16))
        heavy.append((edge * hi).astype(jnp.bfloat16))
        light.append((edge * lo).astype(jnp.bfloat16))
    signs = jnp.concatenate(signs, axis=1)
    matrix = mm(jnp.concatenate(heavy, axis=1), signs, NT)
    matrix = matrix + mm(jnp.concatenate(light, axis=1), signs, NT)
    matrix_ref[:, LANES:] = jnp.zeros_like(matrix_ref[:, LANES:])
    matrix_ref[:, :LANES] = matrix[:, :LANES]
    matrix_ref[:, LANES:ROWS] = matrix[:, LANES:]

    def matrix_rows(k, tile):
        return matrix_ref.at[pl.ds(firsts[k], slot_len), pl.ds(tile * LANES, LANES)]

    def matrix_copy(k, tile, to_chip):
        to_core = side if tile == 0 else core
        owner_core = core if k >= 2 else 1 - core
        return pltpu.make_async_remote_copy(
            src_ref=matrix_rows(k, tile), dst_ref=matrices.at[owner_core, k], send_sem=sent_sem.at[2],
            recv_sem=matrix_sem, device_id=(2 * to_chip + to_core, my_b), device_id_type=MESH,
        )

    owner_chips = [lax.rem(my_w + wide - offset, wide) // 2 for offset in offsets]
    for k in (0, 1, 5):
        @pl.when((k == 5) | (core == 1 - k))
        def _():
            owner_core = core if k >= 2 else 1 - core
            pltpu.make_async_copy(matrix_rows(k, 1), matrices.at[owner_core, k], matrix_sem).start()
            matrix_copy(k, 0, chip).start()

    def send_matrix(wanted):
        for k in range(5):
            @pl.when(wanted(owner_chips[k]))
            def _():
                for tile in range(2):
                    matrix_copy(k, tile, owner_chips[k]).start()

    send_matrix(lambda owner: (owner < chip) & (owner < FIRST))

    def send_both(to_chip):
        far_earlier(to_chip)
        near_copy(to_chip).start()

    loop(FIRST, chip, send_both)
    loop(0, my_b, far_here)
    send_matrix(lambda owner: (owner < chip) & (owner >= FIRST))

    def send_later(which):
        first = which * per_plane
        low = jnp.maximum(first, chip + 1)
        high = first + per_plane
        here = jnp.where(plane == which, blk - 1 - my_b, 0)
        later = jnp.maximum(high - low, 0) * blk + here
        for other in other_chips:
            later = later + jnp.where((other > chip) & (other // per_plane == which), 1, 0)

        @pl.when(later > 0)
        def _():
            pl.semaphore_wait(ready.at[which], later)
            loop(my_b + 1, my_b + 1 + here, lambda to_b: far_copy(chip, to_b).start())

            def one(i):
                to_chip = i
                near_copy(to_chip).start()
                loop(1, blk, lambda step: far_copy(to_chip, lax.rem(my_b + step, blk)).start())

            loop(low, high, one)
            send_matrix(lambda owner: (owner > chip) & (owner // per_plane == which))

    ascending = plane < PLANES // 2

    def plane_at(step):
        late = jnp.where(step < 2, step + 2, step - 2)
        return jnp.where(ascending, step, late)


    def set_targets(which, held):
        columns = held.T
        for k in range(3):
            targets[which, k] = jnp.broadcast_to(columns[:, fields + k:fields + k + 1], (LANES, LANES))

    set_targets(0, own)
    row_id = lax.broadcasted_iota(jnp.int32, (rows, 1), 0)
    factor_row = row_id < fields
    center = jnp.sum(own * area, axis=1, keepdims=True) / jnp.sum(area)
    center = jnp.where(factor_row, center, 0.0)
    vertex_row = lax.broadcasted_iota(jnp.int32, (LANES, LANES), 0).astype(jnp.float32) + 1.0

    def placed(held):
        halves_of = [jnp.where(vertex_row == held[rows + i:rows + i + 1], 1.0, 0.0) for i in range(2)]
        return jnp.concatenate(halves_of, axis=1).astype(jnp.bfloat16)

    acc_ref[...] = jnp.zeros_like(acc_ref)
    sums_ref[...] = jnp.zeros_like(sums_ref)
    pltpu.make_async_copy(near.at[chips], near.at[chips], near_sem.at[PLANES]).wait()
    set_targets(1, near[chips, :rows])
    for step in range(PLANES):
        send_later(plane_at(step))

    def add_pair(source, first):
        his, los, weights = [], [], []
        sums = sums_ref[...]
        for u in range(2):
            block = source[first + u, :rows]
            both = []
            for which in range(2):
                distance = (targets[which, 0] - block[fields:fields + 1]) ** 2
                distance = distance + (targets[which, 1] - block[fields + 1:fields + 2]) ** 2
                distance = distance + (targets[which, 2] - block[fields + 2:fields + 3]) ** 2
                both.append(halves(jnp.log(distance + soften)))
            mass = (block - center) * jnp.where(factor_row, block[fields + 3:], 1.0)
            sums = sums + mass
            his.append(jnp.concatenate([both[0][0], both[1][0]], axis=0))
            los.append(jnp.concatenate([both[0][1], both[1][1]], axis=0))
            weights.append(stacked(mass))
        sums_ref[...] = sums
        weight = jnp.concatenate(weights, axis=1)
        added = mm(weight, jnp.concatenate(his, axis=1), NT)
        acc_ref[...] += added + mm(weight, jnp.concatenate(los, axis=1), NT)

    def near_pair(pair):
        first = 2 * pair
        add_pair(near, first)
        for u in range(2):
            block = near[first + u]
            values[first + u] = mm(stacked(block[:rows]), placed(block), NN)

    def far_plane(which):
        number = (blk - 1) * per_plane
        held = far.at[pl.ds(which * number, number)]
        pltpu.make_async_copy(held, held, far_sem.at[which]).wait()
        loop(which * number // 2, (which + 1) * number // 2, lambda pair: add_pair(far, 2 * pair))

    def one_plane(step):
        which = plane_at(step)
        held = near.at[pl.ds(which * per_plane, per_plane)]
        pltpu.make_async_copy(held, held, near_sem.at[which]).wait()
        loop(which * per_plane // 2, (which + 1) * per_plane // 2, near_pair)

        @pl.when(step + 1 < PLANES)
        def _():
            far_plane(which)

    loop(0, PLANES, one_plane)

    part_lane = lax.broadcasted_iota(jnp.int32, (1, LANES), 1)
    group = [part_lane // slot_len == k for k in range(4)]
    same = [jnp.full((1, LANES), side, jnp.int32) == place for place in range(2)]

    def held_values(owner, tile):
        return values[lax.rem(owner + chips, chips), :, tile * LANES:(tile + 1) * LANES]

    used = {}
    for step, moved in enumerate((0, 1, chips - 1, across)):
        user = chip + moved
        even = jnp.where(group[0], held_values(user - 1, 0), jnp.where(group[1], held_values(user + 1, 0), 0.0))
        even = jnp.where(group[2], held_values(user + across, 0), jnp.where(group[3], held_values(user, 0), even))
        odd = jnp.where(group[0], held_values(user - side, 1), jnp.where(group[1], held_values(user + 1 - side, 1), 0.0))
        for place in range(2):
            used[step, place] = jnp.where(same[place], even, odd).astype(jnp.bfloat16)
    pairs = {
        (0, 0): ((0, 5), (1, 1)), (0, 1): ((0, 0), (1, 5)), (1, 0): ((0, 2), (1, 0)), (1, 1): ((1, 2),),
        (2, 0): ((0, 3),), (2, 1): ((0, 1), (1, 3)), (3, 0): ((0, 4),), (3, 1): ((1, 4),),
    }
    pltpu.make_async_copy(matrices, matrices, matrix_sem).wait()
    returned = {}
    for key, members in pairs.items():
        held = jnp.concatenate([matrices[owner, k] for owner, k in members], axis=0)
        count = held.shape[0]
        hi = held.astype(jnp.bfloat16).astype(jnp.float32)
        both = jnp.concatenate([hi, held - hi], axis=0).astype(jnp.bfloat16)
        result = mm(both, used[key][:rows], NT)
        result = result[:count] + result[count:] + mm(hi.astype(jnp.bfloat16), used[key][rows:], NT)
        for i, member in enumerate(members):
            returned[member] = result[i * slot_len:(i + 1) * slot_len]
    gap = jnp.zeros((LANES - 4 * slot_len, rows), jnp.float32)
    rest = jnp.zeros((LANES - 2 * slot_len, rows), jnp.float32)
    sides = [
        jnp.concatenate(
            [returned[to, k] for k in (2, 3, 4, 5)] + [gap] + [returned[to, k] for k in (0, 1)] + [rest], axis=0
        )
        for to in range(2)
    ]
    first_core = jnp.full((1, rows), core, jnp.int32) == 0
    mine_terms = jnp.where(first_core, sides[0], sides[1])
    other_terms = jnp.where(first_core, sides[1], sides[0])

    def assembled(held, terms):
        place = placed(held)
        hi, lo = halves(terms)
        return (mm(place, hi, NN) + mm(place, lo, NN)).T

    stiffness = assembled(mine_near[...], mine_terms)
    other_stiffness = assembled(near[chips], other_terms)

    far_plane(plane_at(PLANES - 1))

    sums = jnp.sum(sums_ref[...], axis=1, keepdims=True)
    sums = sums + center * sums[fields + 3:]

    def summed(which):
        part = acc_ref[:, which * LANES:(which + 1) * LANES]
        part = part[:rows] + part[rows:]
        return part + center * part[fields + 3:]

    swap[:rows] = summed(1)
    swap[rows:2 * rows] = jnp.broadcast_to(sums, (rows, LANES))
    swap[2 * rows:] = other_stiffness
    swap_copy = pltpu.make_async_remote_copy(
        src_ref=swap, dst_ref=swapped, send_sem=sent_sem.at[3], recv_sem=swap_sem,
        device_id=(sibling, my_b), device_id_type=MESH,
    )
    swap_copy.start()
    own_sum = summed(0)
    sent_far = far.at[pl.ds(0, chips * (blk - 1))]
    pltpu.make_async_copy(sent_far, sent_far, sent_sem.at[0]).wait()
    sent_near = near
    pltpu.make_async_copy(sent_near, sent_near, sent_sem.at[1]).wait()
    for k in range(5):
        pltpu.make_async_copy(matrices.at[:, k], matrices.at[:, k], sent_sem.at[2]).wait()
    swap_copy.wait_recv()
    all_sum = own_sum + swapped[:rows]
    sums = sums + swapped[rows:2 * rows]
    stiffness = stiffness + swapped[2 * rows:]
    shift = sums / sums[fields + 3:]
    long_range = -strength * (all_sum - shift * all_sum[fields + 3:])
    result = stiff_coef * stiffness / area + long_range
    out_ref[...] = result[:fields]
    swap_copy.wait_send()


def per_device(position, order_field, cell_area, slot_vertex, send_count, corner_slot, edge_weight):
    fields, local_count = order_field.shape
    wide, blk = lax.axis_size("wide"), lax.axis_size("blk")
    rows = fields + 4
    chips = wide // 2
    slot_len = slot_vertex.shape[3]
    args = (
        position, order_field, cell_area.reshape(1, local_count), slot_vertex, send_count,
        corner_slot.reshape(3, 1, -1), edge_weight.reshape(3, 1, -1),
    )
    dma = pltpu.SemaphoreType.DMA
    extra = pl.pallas_call(
        functools.partial(kernel, wide, blk, fields, slot_len),
        out_shape=pltpu.VMEM((fields, local_count), jnp.float32),
        in_specs=[pl.BlockSpec(memory_space=pl.ANY)] * 7,
        out_specs=pl.BlockSpec(memory_space=pltpu.VMEM),
        scratch_shapes=[
            *(pltpu.VMEM(x.shape, x.dtype) for x in args),
            pltpu.VMEM((rows, LANES), jnp.float32),
            pltpu.VMEM((rows + ID_ROWS, LANES), jnp.float32),
            pltpu.VMEM((chips + 1, rows + ID_ROWS, LANES), jnp.float32),
            pltpu.VMEM((chips * (blk - 1), rows, LANES), jnp.float32),
            pltpu.VMEM((ROWS, 2 * LANES), jnp.float32),
            pltpu.VMEM((2, 6, slot_len, LANES), jnp.float32),
            pltpu.VMEM((chips, 2 * rows, 2 * LANES), jnp.float32),
            pltpu.VMEM((2, 3, LANES, LANES), jnp.float32),
            pltpu.VMEM((2 * rows, 2 * LANES), jnp.float32),
            pltpu.VMEM((rows, LANES), jnp.float32),
            pltpu.VMEM((3 * rows, LANES), jnp.float32),
            pltpu.VMEM((3 * rows, LANES), jnp.float32),
            dma((7,)), dma((PLANES + 1,)), dma((PLANES,)), dma(()), dma((4,)), dma(()),
            pltpu.SemaphoreType.REGULAR((PLANES,)),
        ],
        compiler_params=pltpu.CompilerParams(collective_id=0, has_side_effects=True),
    )(*args)
    return order_field**3 - order_field + extra


def solution(mesh):
    placed = (
        P(None, ("wide", "blk")),
        P(None, ("wide", "blk")),
        P(("wide", "blk")),
        P("wide", "blk", None, None),
        P("wide", "blk", None),
        P("wide", "blk", None, None),
        P("wide", "blk", None, None),
    )
    return jax.shard_map(
        per_device, mesh=mesh, in_specs=placed, out_specs=P(None, ("wide", "blk")), check_vma=False
    )
```

```python
import functools

import jax
import jax.numpy as jnp
from jax import lax
from jax.experimental import pallas as pl
from jax.experimental.pallas import tpu as pltpu
from jax.sharding import PartitionSpec as P

stiff_coef = 0.1
LANES = 128
PAD = 32
PLANES = 4
FIRST = 1
ID_ROWS = 2
ROWS = 176
MESH = pl.DeviceIdType.MESH
NT = (((1,), (1,)), ((), ()))
NN = (((1,), (0,)), ((), ()))


def halves(x):
    hi = x.astype(jnp.bfloat16)
    lo = (x - hi.astype(jnp.float32)).astype(jnp.bfloat16)
    return hi, lo


def stacked(x):
    return jnp.concatenate(halves(x), axis=0)


def mm(a, b, dims):
    return lax.dot_general(a, b, dims, preferred_element_type=jnp.float32)


def kernel(
    wide, blk, fields, slot_len,
    pos_hbm, order_hbm, area_hbm, slot_hbm, count_hbm, corner_hbm, weight_hbm,
    out_ref,
    pos_ref, order_ref, area_ref, slot_ref, count_ref, corner_ref, weight_ref,
    mine, mine_near, near, far, matrix_ref, matrices, values, targets, acc_ref, sums_ref, swap, swapped,
    load_sem, near_sem, far_sem, matrix_sem, sent_sem, swap_sem, ready,
):
    chips = wide // 2
    across = chips // 2
    per_plane = chips // PLANES
    total = chips * blk
    my_w, my_b = lax.axis_index("wide"), lax.axis_index("blk")
    core, chip = lax.rem(my_w, 2), my_w // 2
    side = 1 - core
    sibling = 2 * chip + side
    plane = chip // per_plane
    place_in_order = chip * blk + my_b
    rows = fields + 4
    soften = 4.0 / (wide * blk * LANES)
    strength = float(wide * blk * LANES) ** (-0.5)
    offsets = (1, wide - 1, 2, wide - 2, wide // 2)
    firsts = (LANES, LANES + slot_len, 0, slot_len, 2 * slot_len, 3 * slot_len)
    steps = (chips - 1, 1, across)

    loads = [
        pltpu.make_async_copy(source, held, load_sem.at[i])
        for i, (source, held) in enumerate((
            (order_hbm, order_ref), (pos_hbm, pos_ref), (area_hbm, area_ref), (slot_hbm, slot_ref),
            (count_hbm, count_ref), (corner_hbm, corner_ref), (weight_hbm, weight_ref),
        ))
    ]
    for load in loads:
        load.start()
    barrier = pltpu.get_barrier_semaphore()

    def device(index):
        return (2 * (index // blk) + side, lax.rem(index, blk))

    def loop(first, last, body):
        def step(i, carry):
            body(i)
            return carry

        lax.fori_loop(first, last, step, 0)

    def signal(semaphore, to):
        pl.semaphore_signal(semaphore, inc=1, device_id=to, device_id_type=MESH)

    other_chips = [lax.rem(chip + step, chips) for step in steps]

    loop(0, total - 1 - place_in_order, lambda i: signal(barrier, device(total - 1 - i)))
    signal(barrier, (sibling, my_b))
    for other in other_chips:
        @pl.when(other > chip)
        def _():
            signal(barrier, (2 * other + core, my_b))

    earlier = place_in_order + 1
    for other in other_chips:
        earlier = earlier + jnp.where(other < chip, 1, 0)
    pl.semaphore_wait(barrier, earlier)

    loop(0, place_in_order, lambda i: signal(ready.at[plane], device(i)))
    for other in other_chips:
        @pl.when(other < chip)
        def _():
            signal(ready.at[plane], (2 * other + core, my_b))

    for load in loads[:3]:
        load.wait()
    own = jnp.concatenate([order_ref[...], pos_ref[...], area_ref[...]], axis=0)
    area = area_ref[...]
    mine[...] = own
    mine_near[:rows] = own

    def far_copy(to_chip, to_b):
        part = lax.rem(my_b - to_b + blk, blk) - 1
        slot = (plane * (blk - 1) + part) * per_plane + chip - plane * per_plane
        return pltpu.make_async_remote_copy(
            src_ref=mine, dst_ref=far.at[slot], send_sem=sent_sem.at[0], recv_sem=far_sem.at[plane],
            device_id=(2 * to_chip + side, to_b), device_id_type=MESH,
        )

    def near_copy(to_chip):
        return pltpu.make_async_remote_copy(
            src_ref=mine_near, dst_ref=near.at[chip], send_sem=sent_sem.at[1], recv_sem=near_sem.at[plane],
            device_id=(2 * to_chip + side, my_b), device_id_type=MESH,
        )

    def far_earlier(to_chip):
        def one(step):
            to_b = lax.rem(my_b + step, blk)
            far_copy(to_chip, to_b).start()

        loop(1, blk, one)

    def far_here(to_b):
        far_copy(chip, to_b).start()

    loop(0, jnp.minimum(chip, FIRST), far_earlier)
    for load in loads[3:5]:
        load.wait()
    lane = lax.broadcasted_iota(jnp.int32, (1, 2 * LANES), 1)
    base = jnp.full((1, 2 * LANES), -1, jnp.int32)
    towards = jnp.full((1, 2 * LANES), -1, jnp.int32)
    for first, offset in zip(firsts, offsets + (0,)):
        inside = (lane >= first) & (lane < first + slot_len)
        base = jnp.where(inside, lane - first, base)
        towards = jnp.where(inside, lax.rem(my_w + offset, wide), towards)
    count_lane = lax.broadcasted_iota(jnp.int32, (wide, wide), 1)
    count_row = lax.broadcasted_iota(jnp.int32, (wide, wide), 0)
    counts = count_ref[0].astype(jnp.float32)
    counts = jnp.sum(jnp.where(count_lane == count_row, counts, 0.0), axis=1, keepdims=True)
    slot_id = lax.broadcasted_iota(jnp.int32, (wide, slot_len), 1).astype(jnp.float32)
    table = jnp.where(slot_id < counts, slot_ref[0, 0].astype(jnp.float32) + 1.0, 0.0)
    spread_row = lax.broadcasted_iota(jnp.int32, (slot_len, 2 * LANES), 0)
    spread = jnp.where(spread_row == base, 1.0, 0.0).astype(jnp.bfloat16)
    spread_table = mm(table.astype(jnp.bfloat16), spread, NN)
    wide_row = lax.broadcasted_iota(jnp.int32, (wide, 2 * LANES), 0)
    vertex_of = jnp.sum(jnp.where(wide_row == towards, spread_table, 0.0), axis=0, keepdims=True)
    mine_near[rows:rows + 1] = vertex_of[:, :LANES]
    mine_near[rows + 1:] = vertex_of[:, LANES:]
    loop(0, jnp.minimum(chip, FIRST), lambda to_chip: near_copy(to_chip).start())
    sibling_copy = pltpu.make_async_remote_copy(
        src_ref=mine_near, dst_ref=near.at[chips], send_sem=sent_sem.at[1], recv_sem=near_sem.at[PLANES],
        device_id=(sibling, my_b), device_id_type=MESH,
    )
    sibling_copy.start()
    near_copy(chip).start()

    for load in loads[5:]:
        load.wait()
    column_id = lax.broadcasted_iota(jnp.int32, (ROWS, corner_ref.shape[2]), 0).astype(jnp.float32).astype(jnp.bfloat16)
    one, zero = jnp.ones((), jnp.bfloat16), jnp.zeros((), jnp.bfloat16)
    picks = []
    for c in range(3):
        corner = corner_ref[c]
        column = jnp.full(corner.shape, -1, jnp.int32)
        for first, offset in zip(firsts, offsets + (0,)):
            low = lax.rem(my_w + wide - offset, wide) * slot_len
            column = jnp.where((corner >= low) & (corner < low + slot_len), corner - low + first, column)
        picks.append(jnp.where(column_id == column.astype(jnp.float32).astype(jnp.bfloat16), one, zero))
    signs, heavy, light = [], [], []
    for c in range(3):
        edge = picks[(c + 1) % 3] - picks[(c + 2) % 3]
        hi, lo = halves(weight_ref[c])
        signs.append(edge)
        heavy.append(edge * hi)
        light.append(edge * lo)
    signs = jnp.concatenate(signs, axis=1)
    matrix = mm(jnp.concatenate(heavy, axis=1), signs, NT)
    matrix = matrix + mm(jnp.concatenate(light, axis=1), signs, NT)
    matrix_ref[:, LANES:] = jnp.zeros_like(matrix_ref[:, LANES:])
    matrix_ref[:, :LANES] = matrix[:, :LANES]
    matrix_ref[:, LANES:ROWS] = matrix[:, LANES:]

    def matrix_rows(k, tile):
        return matrix_ref.at[pl.ds(firsts[k], slot_len), pl.ds(tile * LANES, LANES)]

    def matrix_copy(k, tile, to_chip):
        to_core = side if tile == 0 else core
        owner_core = core if k >= 2 else 1 - core
        return pltpu.make_async_remote_copy(
            src_ref=matrix_rows(k, tile), dst_ref=matrices.at[owner_core, k], send_sem=sent_sem.at[2],
            recv_sem=matrix_sem, device_id=(2 * to_chip + to_core, my_b), device_id_type=MESH,
        )

    owner_chips = [lax.rem(my_w + wide - offset, wide) // 2 for offset in offsets]
    for k in (0, 1, 5):
        @pl.when((k == 5) | (core == 1 - k))
        def _():
            owner_core = core if k >= 2 else 1 - core
            pltpu.make_async_copy(matrix_rows(k, 1), matrices.at[owner_core, k], matrix_sem).start()
            matrix_copy(k, 0, chip).start()

    def send_matrix(wanted):
        for k in range(5):
            @pl.when(wanted(owner_chips[k]))
            def _():
                for tile in range(2):
                    matrix_copy(k, tile, owner_chips[k]).start()

    send_matrix(lambda owner: (owner < chip) & (owner < FIRST))

    def send_both(to_chip):
        far_earlier(to_chip)
        near_copy(to_chip).start()

    loop(FIRST, chip, send_both)
    loop(0, my_b, far_here)
    send_matrix(lambda owner: (owner < chip) & (owner >= FIRST))

    def send_later(which):
        first = which * per_plane
        low = jnp.maximum(first, chip + 1)
        high = first + per_plane
        here = jnp.where(plane == which, blk - 1 - my_b, 0)
        later = jnp.maximum(high - low, 0) * blk + here
        for other in other_chips:
            later = later + jnp.where((other > chip) & (other // per_plane == which), 1, 0)

        @pl.when(later > 0)
        def _():
            pl.semaphore_wait(ready.at[which], later)
            loop(my_b + 1, my_b + 1 + here, lambda to_b: far_copy(chip, to_b).start())

            def one(i):
                to_chip = i
                near_copy(to_chip).start()
                loop(1, blk, lambda step: far_copy(to_chip, lax.rem(my_b + step, blk)).start())

            loop(low, high, one)
            send_matrix(lambda owner: (owner > chip) & (owner // per_plane == which))

    ascending = plane < PLANES // 2

    def plane_at(step):
        late = jnp.where(step < 2, step + 2, step - 2)
        return jnp.where(ascending, step, late)


    def set_targets(which, held):
        columns = held.T
        for k in range(3):
            targets[which, k] = jnp.broadcast_to(columns[:, fields + k:fields + k + 1], (LANES, LANES))

    set_targets(0, own)
    row_id = lax.broadcasted_iota(jnp.int32, (rows, 1), 0)
    factor_row = row_id < fields
    center = jnp.sum(own * area, axis=1, keepdims=True) / jnp.sum(area)
    center = jnp.where(factor_row, center, 0.0)
    vertex_row = lax.broadcasted_iota(jnp.int32, (LANES, LANES), 0).astype(jnp.float32) + 1.0

    def placed(held):
        halves_of = [jnp.where(vertex_row == held[rows + i:rows + i + 1], 1.0, 0.0) for i in range(2)]
        return jnp.concatenate(halves_of, axis=1).astype(jnp.bfloat16)

    acc_ref[...] = jnp.zeros_like(acc_ref)
    sums_ref[...] = jnp.zeros_like(sums_ref)
    pltpu.make_async_copy(near.at[chips], near.at[chips], near_sem.at[PLANES]).wait()
    set_targets(1, near[chips, :rows])
    for step in range(PLANES):
        send_later(plane_at(step))

    def add_pair(source, first):
        his, los, weights = [], [], []
        sums = sums_ref[...]
        for u in range(2):
            block = source[first + u, :rows]
            both = []
            for which in range(2):
                distance = (targets[which, 0] - block[fields:fields + 1]) ** 2
                distance = distance + (targets[which, 1] - block[fields + 1:fields + 2]) ** 2
                distance = distance + (targets[which, 2] - block[fields + 2:fields + 3]) ** 2
                both.append(halves(jnp.log(distance + soften)))
            mass = (block - center) * jnp.where(factor_row, block[fields + 3:], 1.0)
            sums = sums + mass
            his.append(jnp.concatenate([both[0][0], both[1][0]], axis=0))
            los.append(jnp.concatenate([both[0][1], both[1][1]], axis=0))
            weights.append(stacked(mass))
        sums_ref[...] = sums
        weight = jnp.concatenate(weights, axis=1)
        acc_ref[...] += mm(jnp.concatenate([weight, weight], axis=1), jnp.concatenate(his + los, axis=1), NT)

    def near_pair(pair):
        first = 2 * pair
        add_pair(near, first)
        for u in range(2):
            block = near[first + u]
            values[first + u] = mm(stacked(block[:rows]), placed(block), NN)

    def far_plane(which):
        number = (blk - 1) * per_plane
        held = far.at[pl.ds(which * number, number)]
        pltpu.make_async_copy(held, held, far_sem.at[which]).wait()
        loop(which * number // 2, (which + 1) * number // 2, lambda pair: add_pair(far, 2 * pair))

    def one_plane(step):
        which = plane_at(step)
        held = near.at[pl.ds(which * per_plane, per_plane)]
        pltpu.make_async_copy(held, held, near_sem.at[which]).wait()
        loop(which * per_plane // 2, (which + 1) * per_plane // 2, near_pair)

        @pl.when(step + 1 < PLANES)
        def _():
            far_plane(which)

    loop(0, PLANES, one_plane)

    part_lane = lax.broadcasted_iota(jnp.int32, (1, LANES), 1)
    group = [part_lane // slot_len == k for k in range(4)]
    same = [jnp.full((1, LANES), side, jnp.int32) == place for place in range(2)]

    def held_values(owner, tile):
        return values[lax.rem(owner + chips, chips), :, tile * LANES:(tile + 1) * LANES]

    used = {}
    for step, moved in enumerate((0, 1, chips - 1, across)):
        user = chip + moved
        even = jnp.where(group[0], held_values(user - 1, 0), jnp.where(group[1], held_values(user + 1, 0), 0.0))
        even = jnp.where(group[2], held_values(user + across, 0), jnp.where(group[3], held_values(user, 0), even))
        odd = jnp.where(group[0], held_values(user - side, 1), jnp.where(group[1], held_values(user + 1 - side, 1), 0.0))
        for place in range(2):
            used[step, place] = jnp.where(same[place], even, odd).astype(jnp.bfloat16)
    pairs = {
        (0, 0): ((0, 5), (1, 1)), (0, 1): ((0, 0), (1, 5)), (1, 0): ((0, 2), (1, 0)), (1, 1): ((1, 2),),
        (2, 0): ((0, 3),), (2, 1): ((0, 1), (1, 3)), (3, 0): ((0, 4),), (3, 1): ((1, 4),),
    }
    pltpu.make_async_copy(matrices, matrices, matrix_sem).wait()
    returned = {}
    for key, members in pairs.items():
        held = jnp.concatenate([matrices[owner, k] for owner, k in members], axis=0)
        count = held.shape[0]
        hi = held.astype(jnp.bfloat16).astype(jnp.float32)
        both = jnp.concatenate([hi, held - hi], axis=0).astype(jnp.bfloat16)
        result = mm(both, used[key][:rows], NT)
        result = result[:count] + result[count:] + mm(hi.astype(jnp.bfloat16), used[key][rows:], NT)
        for i, member in enumerate(members):
            returned[member] = result[i * slot_len:(i + 1) * slot_len]
    gap = jnp.zeros((LANES - 4 * slot_len, rows), jnp.float32)
    rest = jnp.zeros((LANES - 2 * slot_len, rows), jnp.float32)
    sides = [
        jnp.concatenate(
            [returned[to, k] for k in (2, 3, 4, 5)] + [gap] + [returned[to, k] for k in (0, 1)] + [rest], axis=0
        )
        for to in range(2)
    ]
    first_core = jnp.full((1, rows), core, jnp.int32) == 0
    mine_terms = jnp.where(first_core, sides[0], sides[1])
    other_terms = jnp.where(first_core, sides[1], sides[0])

    def assembled(held, terms):
        place = placed(held)
        hi, lo = halves(terms)
        return (mm(place, hi, NN) + mm(place, lo, NN)).T

    stiffness = assembled(mine_near[...], mine_terms)
    other_stiffness = assembled(near[chips], other_terms)

    far_plane(plane_at(PLANES - 1))

    sums = jnp.sum(sums_ref[...], axis=1, keepdims=True)
    sums = sums + center * sums[fields + 3:]

    def summed(which):
        part = acc_ref[:, which * LANES:(which + 1) * LANES]
        part = part[:rows] + part[rows:]
        return part + center * part[fields + 3:]

    swap[:rows] = summed(1)
    swap[rows:2 * rows] = jnp.broadcast_to(sums, (rows, LANES))
    swap[2 * rows:] = other_stiffness
    swap_copy = pltpu.make_async_remote_copy(
        src_ref=swap, dst_ref=swapped, send_sem=sent_sem.at[3], recv_sem=swap_sem,
        device_id=(sibling, my_b), device_id_type=MESH,
    )
    swap_copy.start()
    own_sum = summed(0)
    sent_far = far.at[pl.ds(0, chips * (blk - 1))]
    pltpu.make_async_copy(sent_far, sent_far, sent_sem.at[0]).wait()
    sent_near = near
    pltpu.make_async_copy(sent_near, sent_near, sent_sem.at[1]).wait()
    for k in range(5):
        pltpu.make_async_copy(matrices.at[:, k], matrices.at[:, k], sent_sem.at[2]).wait()
    swap_copy.wait_recv()
    all_sum = own_sum + swapped[:rows]
    sums = sums + swapped[rows:2 * rows]
    stiffness = stiffness + swapped[2 * rows:]
    shift = sums / sums[fields + 3:]
    long_range = -strength * (all_sum - shift * all_sum[fields + 3:])
    result = stiff_coef * stiffness / area + long_range
    out_ref[...] = result[:fields]
    swap_copy.wait_send()


def per_device(position, order_field, cell_area, slot_vertex, send_count, corner_slot, edge_weight):
    fields, local_count = order_field.shape
    wide, blk = lax.axis_size("wide"), lax.axis_size("blk")
    rows = fields + 4
    chips = wide // 2
    slot_len = slot_vertex.shape[3]
    args = (
        position, order_field, cell_area.reshape(1, local_count), slot_vertex, send_count,
        corner_slot.reshape(3, 1, -1), edge_weight.reshape(3, 1, -1),
    )
    dma = pltpu.SemaphoreType.DMA
    extra = pl.pallas_call(
        functools.partial(kernel, wide, blk, fields, slot_len),
        out_shape=pltpu.VMEM((fields, local_count), jnp.float32),
        in_specs=[pl.BlockSpec(memory_space=pl.ANY)] * 7,
        out_specs=pl.BlockSpec(memory_space=pltpu.VMEM),
        scratch_shapes=[
            *(pltpu.VMEM(x.shape, x.dtype) for x in args),
            pltpu.VMEM((rows, LANES), jnp.float32),
            pltpu.VMEM((rows + ID_ROWS, LANES), jnp.float32),
            pltpu.VMEM((chips + 1, rows + ID_ROWS, LANES), jnp.float32),
            pltpu.VMEM((chips * (blk - 1), rows, LANES), jnp.float32),
            pltpu.VMEM((ROWS, 2 * LANES), jnp.float32),
            pltpu.VMEM((2, 6, slot_len, LANES), jnp.float32),
            pltpu.VMEM((chips, 2 * rows, 2 * LANES), jnp.float32),
            pltpu.VMEM((2, 3, LANES, LANES), jnp.float32),
            pltpu.VMEM((2 * rows, 2 * LANES), jnp.float32),
            pltpu.VMEM((rows, LANES), jnp.float32),
            pltpu.VMEM((3 * rows, LANES), jnp.float32),
            pltpu.VMEM((3 * rows, LANES), jnp.float32),
            dma((7,)), dma((PLANES + 1,)), dma((PLANES,)), dma(()), dma((4,)), dma(()),
            pltpu.SemaphoreType.REGULAR((PLANES,)),
        ],
        compiler_params=pltpu.CompilerParams(collective_id=0, has_side_effects=True),
    )(*args)
    return order_field**3 - order_field + extra


def solution(mesh):
    placed = (
        P(None, ("wide", "blk")),
        P(None, ("wide", "blk")),
        P(("wide", "blk")),
        P("wide", "blk", None, None),
        P("wide", "blk", None),
        P("wide", "blk", None, None),
        P("wide", "blk", None, None),
    )
    return jax.shard_map(
        per_device, mesh=mesh, in_specs=placed, out_specs=P(None, ("wide", "blk")), check_vma=False
    )
```
